32 devices in a mesh: grp: 8 (over z, core), row: 4 (over y, x).
Axes of the slice: x: 2, y: 2, z: 4, core: 2. Of those that a mesh axis runs over, the one named last changes fastest.
Arguments:
- panel_low: bfloat16 [32768, 256], P(('grp', 'row')), may hold values from -6 to 6
- panel_mid: bfloat16 [16384, 256], P(('grp', 'row')), may hold values from -6 to 6
- panel_top: bfloat16 [8192, 256], P(('grp', 'row')), may hold values from -6 to 6
- inverse_low: bfloat16 [2, 32768, 4096], P(None, ('grp', 'row')), may hold values from -0.0625 to 0.0625
- inverse_mid: bfloat16 [2, 16384, 4096], P(None, ('grp', 'row')), may hold values from -0.0625 to 0.0625
- inverse_top: bfloat16 [2, 8192, 4096], P(None, ('grp', 'row')), may hold values from -0.0625 to 0.0625
- couple_low: bfloat16 [2, 2048, 32768], P(None, None, ('grp', 'row')), may hold values from -0.0625 to 0.0625
- couple_mid: bfloat16 [2, 2048, 16384], P(None, None, ('grp', 'row')), may hold values from -0.0625 to 0.0625
- parents_low: int32 [8, 2048], replicated, may hold values from 0 to 4095, as said below
- parents_mid: int32 [4, 2048], replicated, may hold values from 0 to 4095, as said below
Outputs:
- solution_low: float32 [32768, 256], P(('grp', 'row'))
- solution_mid: float32 [16384, 256], P(('grp', 'row'))
- solution_top: float32 [8192, 256], P(('grp', 'row'))
The draws below stay inside these ranges and needn't reach their ends.
Inputs may be any that keep to these rules, and one draw needn't show every extreme that they name: `parents_low`: each row holds 2048 distinct row numbers of the parent front. `parents_mid`: each row holds 2048 distinct row numbers of the parent front.
All inputs are finite; a program needn't handle non-finite values.
Results may differ from the reference program's by a relative error of at most 0.024.
Values may be sent and summed in bfloat16 or wider, within the bound.
A program may use at most 128 MiB of HBM per device.

```python
import jax
import jax.numpy as jnp
from jax import lax

F = 4096
K = 2048
R = 128
NLOW = 8
NMID = 4
NTOP = 2


def target_rows(key, count):

    def one_front(front_key):
        key_hot, key_score = jax.random.split(front_key)
        hot_blocks = jax.random.randint(key_hot, (16,), 0, 2)
        weights = 1 + 3 * jnp.repeat(hot_blocks, F // 16)
        scores = jax.random.randint(key_score, (F,), 0, 1024) * weights
        order = jnp.argsort(-(scores * F + jnp.arange(F)))
        return order[:K].astype(jnp.int32)
    keys = jax.random.split(key, count)
    rows = jax.vmap(one_front)(keys)
    chosen = jax.random.randint(jax.random.fold_in(key, 7), (), 0, count)
    ends = jnp.array([F - 1, 0], dtype=jnp.int32)
    middle = 1 + jax.random.permutation(jax.random.fold_in(key, 11), F - 2).astype(jnp.int32)
    forced = jnp.concatenate([ends, middle[:K - 2]])
    forced = jax.random.permutation(jax.random.fold_in(key, 13), forced)
    rows = jnp.where(jnp.arange(count)[:, None] == chosen, forced[None, :], rows)
    return rows.astype(jnp.int32)


def draw_parents_low(key, part):
    return target_rows(jax.random.fold_in(key, 101), NLOW)


def draw_parents_mid(key, part):
    return target_rows(jax.random.fold_in(key, 202), NMID)


def levels(rng, extent, pieces, low, largest):
    gain = 1.0
    for dim, shards_of in pieces:
        steps = jax.random.uniform(jax.random.fold_in(jax.random.fold_in(rng, 6), dim), (shards_of,), jnp.float32, low / len(pieces), largest / len(pieces))
        gain = gain * jnp.repeat(jnp.exp(steps), extent[dim] // shards_of).reshape((-1,) + (1,) * (len(extent) - 1 - dim))
    return gain


def normal_values(key, dims, scale, limit, shards=(), kind=jnp.bfloat16):
    factor_of = levels(key, dims, shards, -0.22, 0.18) if shards else 1.0
    result = jax.random.normal(key, dims, jnp.float32) * scale * factor_of
    return jnp.minimum(jnp.maximum(result, -limit), limit).astype(kind)


def setup_inputs(seed: int = 0) -> dict:
    streams_of = jax.random.split(jax.random.key(seed), 11)
    panel_low = normal_values(streams_of[0], (NLOW * F, 2 * R), 1.0, 6.0, ((0, 32),))
    panel_mid = normal_values(streams_of[1], (NMID * F, 2 * R), 1.0, 6.0, ((0, 32),))
    panel_top = normal_values(streams_of[2], (NTOP * F, 2 * R), 1.0, 6.0, ((0, 32),))
    inverse_low = normal_values(streams_of[3], (2, NLOW * F, F), (2 * F) ** -0.5, 0.0625, ((1, 32),))
    inverse_mid = normal_values(streams_of[4], (2, NMID * F, F), (2 * F) ** -0.5, 0.0625, ((1, 32),))
    inverse_top = normal_values(streams_of[5], (2, NTOP * F, F), (2 * F) ** -0.5, 0.0625, ((1, 32),))
    couple_low = normal_values(streams_of[6], (2, K, NLOW * F), (2 * F) ** -0.5, 0.0625, ((2, 32),))
    couple_mid = normal_values(streams_of[7], (2, K, NMID * F), (2 * F) ** -0.5, 0.0625, ((2, 32),))
    parents_low = draw_parents_low(jax.random.fold_in(streams_of[10], 71), 0)
    parents_mid = draw_parents_mid(jax.random.fold_in(streams_of[10], 71), 0)
    return {"panel_low": panel_low, "panel_mid": panel_mid, "panel_top": panel_top, "inverse_low": inverse_low, "inverse_mid": inverse_mid, "inverse_top": inverse_top, "couple_low": couple_low, "couple_mid": couple_mid, "parents_low": parents_low, "parents_mid": parents_mid}


def complex_product(matrix, panel):
    width = panel.shape[1] // 2
    real_term = jnp.dot(matrix[0], panel, preferred_element_type=jnp.float32)
    imag_term = jnp.dot(matrix[1], panel, preferred_element_type=jnp.float32)
    return real_term + jnp.concatenate([-imag_term[:, width:], imag_term[:, :width]], axis=1)


def transposed_product(matrix, panel):
    width = panel.shape[1] // 2
    real_term = jnp.dot(matrix[0].T, panel, preferred_element_type=jnp.float32)
    imag_term = jnp.dot(matrix[1].T, panel, preferred_element_type=jnp.float32)
    return real_term + jnp.concatenate([-imag_term[:, width:], imag_term[:, :width]], axis=1)


def split_inverse(matrix, count):
    return matrix.reshape(2, count, F, F).transpose(1, 0, 2, 3)


def split_couple(matrix, count):
    return matrix.reshape(2, K, count, F).transpose(2, 0, 1, 3)


def solve_each(pair):
    return complex_product(pair[0], pair[1])


def assemble(parent_panel, parts, targets, count):
    def scatter_one(pair):
        return jnp.zeros((F, 2 * R), jnp.float32).at[pair[0]].add(pair[1])

    spread = lax.map(scatter_one, (targets, parts))
    summed = spread.reshape(count, 2, F, 2 * R).sum(axis=1)
    return (parent_panel.astype(jnp.float32) - summed).astype(jnp.bfloat16)


def descend(parent_x, targets, couples, inverses, own_y):
    upper = jnp.repeat(parent_x.astype(jnp.bfloat16), 2, axis=0)

    def one_front(items):
        up_panel, rows, couple, inverse, own = items
        picked = up_panel[rows]
        lifted = transposed_product(couple, picked).astype(jnp.bfloat16)
        return own - complex_product(inverse, lifted)

    return lax.map(one_front, (upper, targets, couples, inverses, own_y))


def reference(panel_low, panel_mid, panel_top, inverse_low, inverse_mid, inverse_top, couple_low, couple_mid, parents_low, parents_mid):
    inv_lowest = split_inverse(inverse_low, NLOW)
    inv_middle = split_inverse(inverse_mid, NMID)
    inv_upper = split_inverse(inverse_top, NTOP)
    cpl_lowest = split_couple(couple_low, NLOW)
    cpl_middle = split_couple(couple_mid, NMID)
    low_y = lax.map(solve_each, (inv_lowest, panel_low.reshape(NLOW, F, 2 * R)))
    low_part = lax.map(solve_each, (cpl_lowest, low_y.astype(jnp.bfloat16)))
    mid_right = assemble(panel_mid.reshape(NMID, F, 2 * R), low_part, parents_low, NMID)
    mid_y = lax.map(solve_each, (inv_middle, mid_right))
    mid_part = lax.map(solve_each, (cpl_middle, mid_y.astype(jnp.bfloat16)))
    top_right = assemble(panel_top.reshape(NTOP, F, 2 * R), mid_part, parents_mid, NTOP)
    top_x = lax.map(solve_each, (inv_upper, top_right))
    mid_x = descend(top_x, parents_mid, cpl_middle, inv_middle, mid_y)
    low_x = descend(mid_x, parents_low, cpl_lowest, inv_lowest, low_y)
    return (low_x.reshape(NLOW * F, 2 * R), mid_x.reshape(NMID * F, 2 * R), top_x.reshape(NTOP * F, 2 * R))
```

```python
import functools

import jax
import jax.numpy as jnp
from jax import lax
from jax.experimental import pallas as pl
from jax.experimental.pallas import tpu as pltpu
from jax.sharding import PartitionSpec as P

F = 4096
MESH = pl.DeviceIdType.MESH


def complex_product(matrix, panel):
    width = panel.shape[1] // 2
    real_term = jnp.dot(matrix[0], panel, preferred_element_type=jnp.float32)
    imag_term = jnp.dot(matrix[1], panel, preferred_element_type=jnp.float32)
    return real_term + jnp.concatenate([-imag_term[:, width:], imag_term[:, :width]], axis=1)


def transposed_product(matrix, panel):
    width = panel.shape[1] // 2
    contract = (((0,), (0,)), ((), ()))
    real_term = lax.dot_general(matrix[0], panel, contract, preferred_element_type=jnp.float32)
    imag_term = lax.dot_general(matrix[1], panel, contract, preferred_element_type=jnp.float32)
    return real_term + jnp.concatenate([-imag_term[:, width:], imag_term[:, :width]], axis=1)


class Place:
    def __init__(self, n, levels):
        self.n = n
        self.levels = levels
        self.square = n == 4
        self.group = lax.axis_index("grp")
        self.row = lax.axis_index("row")
        self.core = lax.rem(self.group, 2)
        self.upper = lax.rem(self.group // 2, 2)
        self.partner = (self.group + 1 - 2 * self.core, self.row)
        self.across = (self.group + 2 - 4 * self.upper, self.row)
        self.unit = lax.rem(self.group, 2**levels)
        if self.square:
            side = self.row + 1 - 2 * lax.rem(self.row, 2)
            over = self.row + 2 - 4 * (self.row // 2)
            self.ring = [self.row, side, over, 3 - self.row]
            self.side = (self.group, side)
            self.over = (self.group, over)

    def ahead(self, step):
        return self.ring[step] if self.square else lax.rem(self.row + step, self.n)

    def behind(self, step):
        return self.ring[step] if self.square else lax.rem(self.row + self.n - step, self.n)

    def greet(self):
        barrier = pltpu.get_barrier_semaphore()
        if self.square:
            peers = [self.side, self.over]
        else:
            peers = [(self.group, self.ahead(s)) for s in range(1, self.n)]
        if self.levels >= 1:
            peers.append(self.partner)
        if self.levels >= 2:
            peers.append(self.across)
        for peer in peers:
            pl.semaphore_signal(barrier, inc=1, device_id=peer, device_id_type=MESH)
        pl.semaphore_wait(barrier, len(peers))


def push(src, dst, send, recv, peer):
    return pltpu.make_async_remote_copy(
        src_ref=src, dst_ref=dst, send_sem=send, recv_sem=recv, device_id=peer, device_id_type=MESH
    )


def half_of(ref, index):
    rows = ref.shape[0] // 2
    return ref.at[pl.ds(index * rows, rows)]


def spread(at, out, sems, use):
    n, levels = at.n, at.levels
    row_send, row_recv, pair_send, pair_recv, z_send, z_recv = sems
    near = at.unit
    started = []

    def go(src, send, recv, peer):
        copy = push(src, src, send, recv, peer)
        copy.start()
        started.append(copy)

    def landed(ref, send, recv, peer):
        push(ref, ref, send, recv, peer).wait_recv()

    def row_copy(act, which, k, slot, half, peer):
        act(half_of(out.at[slot], half), row_send.at[which, k], row_recv.at[which, k], peer)

    def to_rows(which, unit):
        mine = unit * n + at.row
        if at.square:
            row_copy(go, which, 0, mine, 0, at.side)
            row_copy(go, which, 1, mine, 1, at.over)
            row_copy(go, which, 2, mine, 1, at.side)
            row_copy(go, which, 3, mine, 0, at.over)
            return
        for s in range(1, n):
            go(out.at[mine], row_send.at[which, s], row_recv.at[which, s], (at.group, at.ahead(s)))

    def forward(which, unit):
        if at.square:
            side, over = unit * n + at.ring[1], unit * n + at.ring[2]
            row_copy(landed, which, 0, side, 0, at.side)
            row_copy(go, which, 4, side, 0, at.over)
            row_copy(landed, which, 1, over, 1, at.over)
            row_copy(go, which, 5, over, 1, at.side)

    def await_row(which, unit, s):
        slot = unit * n + at.behind(s)
        if not at.square:
            peer = (at.group, at.behind(s))
            landed(out.at[slot], row_send.at[which, s], row_recv.at[which, s], peer)
        elif s == 1:
            row_copy(landed, which, 2, slot, 1, at.side)
        elif s == 2:
            row_copy(landed, which, 3, slot, 0, at.over)
        else:
            row_copy(landed, which, 4, slot, 0, at.over)
            row_copy(landed, which, 5, slot, 1, at.side)

    def to_pair(which, s, unit):
        src = out.at[unit * n + at.behind(s)]
        go(src, pair_send.at[which, s], pair_recv.at[which, s], at.partner)

    def await_pair(which, s, unit):
        slot = (unit + 1 - 2 * at.core) * n + at.behind(s)
        landed(out.at[slot], pair_send.at[which, s], pair_recv.at[which, s], at.partner)
        use(slot)

    units = [near]
    if levels >= 2:
        units.append(lax.rem(near + 2, 4))
        go(out.at[near * n + at.row], z_send.at[0], z_recv.at[0], at.across)
    to_rows(0, near)
    if levels >= 1:
        to_pair(0, 0, near)
    if levels >= 2:
        landed(out.at[units[1] * n + at.row], z_send.at[0], z_recv.at[0], at.across)
        to_rows(1, units[1])
        to_pair(1, 0, units[1])
    use(near * n + at.row)
    if levels >= 2:
        use(units[1] * n + at.row)
    for which, unit in enumerate(units):
        forward(which, unit)
    for s in range(1, n):
        for which, unit in enumerate(units):
            await_row(which, unit, s)
            if levels >= 1:
                to_pair(which, s, unit)
                await_pair(which, s - 1, unit)
            use(unit * n + at.behind(s))
    if levels >= 1:
        for which, unit in enumerate(units):
            await_pair(which, n - 1, unit)
    for copy in started:
        copy.wait_send()


def solver(n, out, inverse_hbm, inverse, turned, total, sem):
    count, block, width = out.shape
    rows = inverse.shape[1]
    tile = min(rows, 256)
    whole = block % 128 == 0
    together = 1 if whole else turned.shape[0] // block
    copy = pltpu.make_async_copy(inverse_hbm, inverse, sem)
    copy.start()
    waiting = [copy]

    def multiply(slot, first):
        panel = out[slot] if whole else out[pl.ds(slot, together)].reshape(turned.shape)
        half = width // 2
        turned[:, :half] = -panel[:, half:]
        turned[:, half:] = panel[:, :half]
        span_columns = turned.shape[0]
        columns = pl.ds(pl.multiple_of(slot // together * span_columns, span_columns), span_columns)

        def body(index, carry):
            span = pl.ds(pl.multiple_of(index * tile, tile), tile)
            block_now = out[slot] if whole else panel
            real = jnp.dot(inverse[0, span, columns], block_now, preferred_element_type=jnp.float32)
            imag = jnp.dot(inverse[1, span, columns], turned[...], preferred_element_type=jnp.float32)
            if first:
                total[span, :] = real + imag
            else:
                total[span, :] = total[span, :] + (real + imag)
            return carry

        lax.fori_loop(0, rows // tile, body, 0)

    def use(slot):
        if whole:
            first = bool(waiting)
            if first:
                waiting.pop().wait()
            multiply(slot, first)

    def rest():
        if not whole:
            waiting.pop().wait()
            for slot in range(0, count, together):
                multiply(slot, slot == 0)

    return use, rest


def gather_kernel(n, levels, own, full, *sems):
    at = Place(n, levels)
    at.greet()
    full[at.unit * n + at.row] = own[...]
    spread(at, full, sems, lambda slot: None)


def gather_solve_kernel(n, levels, own, inverse_hbm, total, full, inverse, turned, sem, *sems):
    at = Place(n, levels)
    use, rest = solver(n, full, inverse_hbm, inverse, turned, total, sem)
    at.greet()
    full[at.unit * n + at.row] = own[...]
    spread(at, full, sems, use)
    rest()


def add_rows(out_ref, terms, panel=None):
    rows = out_ref.shape[0]
    step = min(rows, 64)

    def body(index, carry):
        span = pl.ds(pl.multiple_of(index * step, step), step)
        total = terms[0][span, :].astype(jnp.float32)
        for term in terms[1:]:
            total = total + term[span, :].astype(jnp.float32)
        if panel is not None:
            total = panel[span, :].astype(jnp.float32) - total
        out_ref[span, :] = total.astype(out_ref.dtype)
        return carry

    lax.fori_loop(0, rows // step, body, 0)


def reduce_solve_kernel(
    n, levels, term, panel, inverse_hbm, total, full, inverse, turned, near_buf, stage, row_buf, z_buf, sem, *sems
):
    at = Place(n, levels)
    halves = 2 ** (levels - 1)
    spread_sems = sems[:6]
    pair_send, pair_recv, row_send, row_recv, z_send, z_recv = sems[6:]
    use, finish_solve = solver(n, full, inverse_hbm, inverse, turned, total, sem)
    at.greet()
    started = []

    def go(src, dst, send, recv, peer):
        copy = push(src, dst, send, recv, peer)
        copy.start()
        started.append(copy)

    def landed(ref, send, recv, peer):
        push(ref, ref, send, recv, peer).wait_recv()

    order = [3, 1, 2, 0] if at.square else list(range(1, n)) + [0]
    for s in order:
        for half in range(halves):
            src = term.at[(half * 2 + 1 - at.core) * n + at.ahead(s)]
            go(src, near_buf.at[half, s], pair_send.at[half, s], pair_recv.at[half, s], at.partner)

    def own_term(half, s):
        return term.at[(half * 2 + at.core) * n + at.ahead(s)]

    def await_pair(half, s):
        landed(near_buf.at[half, s], pair_send.at[half, s], pair_recv.at[half, s], at.partner)

    def row_copy(half, k, src, peer):
        go(src, row_buf.at[half, k], row_send.at[half, k], row_recv.at[half, k], peer)

    def await_row(half, k, peer):
        landed(row_buf.at[half, k], row_send.at[half, k], row_recv.at[half, k], peer)

    if at.square:
        for half in range(halves):
            await_pair(half, 3)
            add_rows(stage.at[half, 3], [own_term(half, 3), near_buf.at[half, 3]])
            row_copy(half, 0, half_of(stage.at[half, 3], 0), at.side)
            row_copy(half, 3, half_of(stage.at[half, 3], 1), at.over)
        for half in range(halves):
            await_pair(half, 1)
            first = half_of(stage.at[half, 1], 0)
            add_rows(first, [half_of(own_term(half, 1), 0), half_of(near_buf.at[half, 1], 0)])
            row_copy(half, 1, first, at.side)
            await_pair(half, 2)
            second = half_of(stage.at[half, 2], 1)
            add_rows(second, [half_of(own_term(half, 2), 1), half_of(near_buf.at[half, 2], 1)])
            row_copy(half, 4, second, at.over)
        for half in range(halves):
            await_row(half, 0, at.side)
            first = half_of(stage.at[half, 2], 0)
            near = half_of(near_buf.at[half, 2], 0)
            add_rows(first, [half_of(own_term(half, 2), 0), near, row_buf.at[half, 0]])
            row_copy(half, 2, first, at.over)
            await_row(half, 3, at.over)
            second = half_of(stage.at[half, 1], 1)
            near = half_of(near_buf.at[half, 1], 1)
            add_rows(second, [half_of(own_term(half, 1), 1), near, row_buf.at[half, 3]])
            row_copy(half, 5, second, at.side)
        for half in range(halves):
            await_pair(half, 0)
            await_row(half, 1, at.side)
            await_row(half, 4, at.over)
            await_row(half, 2, at.over)
            await_row(half, 5, at.side)
    else:
        for s in range(1, n):
            for half in range(halves):
                await_pair(half, s)
                add_rows(stage.at[half, s], [own_term(half, s), near_buf.at[half, s]])
                row_copy(half, s, stage.at[half, s], (at.group, at.ahead(s)))
        for half in range(halves):
            await_pair(half, 0)
            for s in range(1, n):
                await_row(half, s, (at.group, at.behind(s)))

    def finish(dst, half, extra, base):
        own, near = own_term(half, 0), near_buf.at[half, 0]
        if not at.square:
            rest = [row_buf.at[half, s] for s in range(1, n)]
            add_rows(dst, [own, near] + rest + extra, base)
            return
        for part in range(2):
            rest = [row_buf.at[half, 1 + 3 * part], row_buf.at[half, 2 + 3 * part]]
            rest = rest + [half_of(ref, part) for ref in extra]
            terms = [half_of(own, part), half_of(near, part)] + rest
            add_rows(half_of(dst, part), terms, None if base is None else half_of(base, part))

    slot = at.unit * n + at.row
    if levels == 1:
        finish(full.at[slot], 0, [], panel)
    else:
        finish(z_buf.at[0], 1 - at.upper, [], None)
        go(z_buf.at[0], z_buf.at[1], z_send.at[0], z_recv.at[0], at.across)
        landed(z_buf.at[1], z_send.at[0], z_recv.at[0], at.across)
        finish(full.at[slot], at.upper, [z_buf.at[1]], panel)
    spread(at, full, spread_sems, use)
    finish_solve()
    for copy in started:
        copy.wait_send()


def dma(*shape):
    return pltpu.SemaphoreType.DMA(shape)


VMEM_SPEC = pl.BlockSpec(memory_space=pltpu.VMEM)
HBM_SPEC = pl.BlockSpec(memory_space=pltpu.HBM)


def spread_scratch(n):
    k = max(n, 6)
    return [dma(2, k), dma(2, k), dma(2, n), dma(2, n), dma(1), dma(1)]


def params(ident, mebibytes):
    return pltpu.CompilerParams(
        collective_id=ident, has_side_effects=True, vmem_limit_bytes=mebibytes << 20
    )


def gather(own, n, levels, ident):
    block, width = own.shape
    count = 2**levels * n
    full = pl.pallas_call(
        functools.partial(gather_kernel, n, levels),
        out_shape=jax.ShapeDtypeStruct((count, block, width), own.dtype),
        in_specs=[VMEM_SPEC],
        out_specs=VMEM_SPEC,
        scratch_shapes=spread_scratch(n),
        compiler_params=params(ident, 16),
    )(own)
    return full.reshape(count * block, width)


def solve_scratch(inverse, block, width, count):
    return [
        pltpu.VMEM((count, block, width), jnp.bfloat16),
        pltpu.VMEM(inverse.shape, inverse.dtype),
        pltpu.VMEM((block if block % 128 == 0 else 512, width), jnp.bfloat16),
    ]


def gather_solve(own, inverse, n, levels, ident):
    block, width = own.shape
    return pl.pallas_call(
        functools.partial(gather_solve_kernel, n, levels),
        out_shape=jax.ShapeDtypeStruct((inverse.shape[1], width), jnp.float32),
        in_specs=[VMEM_SPEC, HBM_SPEC],
        out_specs=VMEM_SPEC,
        scratch_shapes=solve_scratch(inverse, block, width, 2**levels * n)
        + [pltpu.SemaphoreType.DMA]
        + spread_scratch(n),
        compiler_params=params(ident, 32),
    )(own, inverse)


def reduce_solve(term, panel, inverse, n, levels, ident):
    block, width = panel.shape
    count = 2**levels * n
    halves = 2 ** (levels - 1)
    whole = pltpu.VMEM((halves, n, block, width), jnp.bfloat16)
    if n == 4:
        pieces, k = pltpu.VMEM((halves, 6, block // 2, width), jnp.bfloat16), 6
    else:
        pieces, k = whole, n
    return pl.pallas_call(
        functools.partial(reduce_solve_kernel, n, levels),
        out_shape=jax.ShapeDtypeStruct((inverse.shape[1], width), jnp.float32),
        in_specs=[VMEM_SPEC, VMEM_SPEC, HBM_SPEC],
        out_specs=VMEM_SPEC,
        scratch_shapes=solve_scratch(inverse, block, width, count)
        + [whole, whole, pieces, pltpu.VMEM((2, block, width), jnp.bfloat16)]
        + [pltpu.SemaphoreType.DMA]
        + spread_scratch(n)
        + [dma(halves, n), dma(halves, n), dma(halves, k), dma(halves, k), dma(1), dma(1)],
        compiler_params=params(ident, 32),
    )(term.reshape(count, block, width), panel, inverse)


def spread_kernel(tile, targets, rows, out):
    index = lax.broadcasted_iota(jnp.int32, (tile, 1), 0) + pl.program_id(0) * tile
    marks = (index == targets[...]).astype(jnp.float32).astype(jnp.bfloat16)
    out[...] = jnp.dot(marks, rows[...], preferred_element_type=jnp.float32).astype(out.dtype)


def spread_rows(partial_rows, targets):
    count, width = partial_rows.shape
    tile = F // 4
    return pl.pallas_call(
        functools.partial(spread_kernel, tile),
        grid=(F // tile,),
        in_specs=[
            pl.BlockSpec((1, count), lambda i: (0, 0)),
            pl.BlockSpec((count, width), lambda i: (0, 0)),
        ],
        out_specs=pl.BlockSpec((tile, width), lambda i: (i, 0)),
        out_shape=jax.ShapeDtypeStruct((F, width), jnp.bfloat16),
        compiler_params=pltpu.CompilerParams(vmem_limit_bytes=32 << 20),
    )(targets[None, :], partial_rows.astype(jnp.bfloat16))


def pick_rows(panel, targets):
    marks = (targets[:, None] == lax.broadcasted_iota(jnp.int32, (1, F), 1)).astype(jnp.bfloat16)
    return jnp.dot(marks, panel, preferred_element_type=jnp.float32).astype(jnp.bfloat16)


def dot32(left, right):
    return jnp.dot(left, right, preferred_element_type=jnp.float32)


def turn(product):
    half, width = product.shape[0] // 2, product.shape[1] // 2
    real, imag = product[:half], product[half:]
    return real + jnp.concatenate([-imag[:, width:], imag[:, :width]], axis=1)


def rows_at(ref, start, count):
    return ref.at[pl.ds(pl.multiple_of(start, count), count)]


def multiply(matrix, panel, total, start, depth, sign, first=False):
    rows = matrix.shape[1]
    tile = min(rows, 512)
    span = pl.ds(pl.multiple_of(start, depth), depth)
    block = panel[span, :]
    for base in range(0, rows, tile):
        part = pl.ds(base, tile)
        left = matrix[:, part, span].reshape(2 * tile, depth)
        product = turn(dot32(left, block))
        if first:
            total[part, :] = product
        elif sign > 0:
            total[part, :] = total[part, :] + product
        else:
            total[part, :] = total[part, :] - product


def couple_rows(matrix, panel, out):
    tile = 1024
    for base in range(0, matrix.shape[1], tile):
        part = pl.ds(base, tile)
        left = matrix[:, part, :].reshape(2 * tile, matrix.shape[2])
        out[part, :] = turn(dot32(left, panel)).astype(out.dtype)


def lift_rows(matrix, panel, start, count):
    columns = pl.ds(start, count)
    contract = (((0,), (0,)), ((), ()))
    real = lax.dot_general(matrix[0, :, columns], panel, contract, preferred_element_type=jnp.float32)
    imag = lax.dot_general(matrix[1, :, columns], panel, contract, preferred_element_type=jnp.float32)
    width = panel.shape[1] // 2
    return real + jnp.concatenate([-imag[:, width:], imag[:, :width]], axis=1)


def place_rows(term, part, targets, starts, count):
    iota = lax.broadcasted_iota(jnp.int32, (count, 1), 0)
    marks = [(iota + start == targets).astype(jnp.float32).astype(jnp.bfloat16) for start in starts]
    placed = dot32(jnp.concatenate(marks, axis=0), part[...])
    for index, start in enumerate(starts):
        rows_at(term, start, count)[...] = placed[index * count : (index + 1) * count].astype(term.dtype)


def spread_lanes(wide, targets):
    for base in range(0, wide.shape[0], 128):
        square = jnp.broadcast_to(targets[:, base : base + 128], (128, 128))
        wide[pl.ds(base, 128), :] = square.T


def pick_add(total, wide, panel, starts, depth, first=False):
    blocks = [panel[pl.ds(pl.multiple_of(start, depth), depth), :] for start in starts]
    block = jnp.concatenate(blocks, axis=0) if len(blocks) > 1 else blocks[0]
    lanes = lax.broadcasted_iota(jnp.int32, (1, 128), 1)
    tile = 1024
    for base in range(0, wide.shape[0], tile):
        part = pl.ds(base, tile)
        wanted = wide[part, :]
        marks = []
        for start in starts:
            for shift in range(0, depth, 128):
                marks.append((lanes + (start + shift) == wanted).astype(jnp.float32).astype(jnp.bfloat16))
        product = dot32(jnp.concatenate(marks, axis=1), block)
        total[part, :] = product if first else total[part, :] + product


def add_all(out, terms, base=None):
    total = terms[0][...].astype(jnp.float32)
    for term in terms[1:]:
        total = total + term[...].astype(jnp.float32)
    if base is not None:
        total = base[...].astype(jnp.float32) - total
    out[...] = total.astype(out.dtype)


class Sender:
    def __init__(self):
        self.started = []

    def go(self, src, dst, send, recv, peer):
        copy = push(src, dst, send, recv, peer)
        copy.start()
        self.started.append(copy)

    def finish(self):
        for copy in self.started:
            copy.wait_send()
        self.started = []


class Exchange(Sender):
    def __init__(self, at, buf, levels, sub, sems, source=None):
        super().__init__()
        self.at, self.buf, self.levels, self.sub = at, buf, levels, sub
        self.row_send, self.row_recv, self.pair_send, self.pair_recv, self.z_send, self.z_recv = sems
        self.block = buf.shape[0] // (4 * 2**levels)
        self.pieces = 2 * sub
        self.count = self.block // self.pieces
        self.source = source
        near = lax.rem(at.group, 2**levels)
        self.units = [near]
        if levels >= 2:
            self.units.append(lax.rem(near + 2, 4))
        self.mine = self.start_of(near, 0)

    def start_of(self, unit, s):
        return (unit * 4 + self.at.ring[s]) * self.block

    def starts(self, s):
        return [self.start_of(unit, s) for unit in self.units]

    def pair_starts(self, s):
        return [self.start_of(unit + 1 - 2 * self.at.core, s) for unit in self.units]

    def piece(self, which, s, p):
        return rows_at(self.buf, self.start_of(self.units[which], s) + p * self.count, self.count)

    def row_act(self, act, which, link, stage, index, ref, src=None):
        k = (link * 3 + stage) * self.sub + index
        peer = self.at.over if link else self.at.side
        act(ref if src is None else src, ref, self.row_send.at[which, k], self.row_recv.at[which, k], peer)

    def pair_act(self, act, which, s, p, ref, src=None):
        k = s * self.pieces + p
        act(ref if src is None else src, ref, self.pair_send.at[which, k], self.pair_recv.at[which, k], self.at.partner)

    def landed(self, src, dst, send, recv, peer):
        push(dst, dst, send, recv, peer).wait_recv()

    def send_piece(self, which, p):
        ref = self.piece(which, 0, p)
        src = None
        if self.source is not None:
            src = self.source.at[pl.ds(p * self.count, self.count)]
        half, index = p // self.sub, p % self.sub
        if half == 0:
            self.row_act(self.go, which, 0, 0, index, ref, src)
            self.row_act(self.go, which, 1, 1, index, ref, src)
        else:
            self.row_act(self.go, which, 1, 0, index, ref, src)
            self.row_act(self.go, which, 0, 1, index, ref, src)
        if self.levels >= 2 and which == 0:
            self.go(ref, ref, self.z_send.at[p], self.z_recv.at[p], self.at.across)
        if self.levels >= 1:
            self.pair_act(self.go, which, 0, p, ref, src)

    def relay_z(self):
        for p in range(self.pieces):
            ref = self.piece(1, 0, p)
            self.landed(ref, ref, self.z_send.at[p], self.z_recv.at[p], self.at.across)
            self.send_piece(1, p)

    def arrive(self, which, link, stage, index):
        if stage == 2:
            s, half = 3, 1 - link
            half = 0 if link else 1
        else:
            s = 2 if link else 1
            half = (0 if stage == 0 else 1) if link == 0 else (1 if stage == 0 else 0)
        p = half * self.sub + index
        ref = self.piece(which, s, p)
        self.row_act(self.landed, which, link, stage, index, ref)
        if stage == 0:
            self.row_act(self.go, which, 1 - link, 2, index, ref)
        if self.levels >= 1:
            self.pair_act(self.go, which, s, p, ref)

    def arrive_stage(self, stage):
        for which in range(len(self.units)):
            for index in range(self.sub):
                for link in range(2):
                    self.arrive(which, link, stage, index)

    def await_pair(self, s):
        for which, unit in enumerate(self.units):
            for p in range(self.pieces):
                start = self.start_of(unit + 1 - 2 * self.at.core, s) + p * self.count
                ref = rows_at(self.buf, start, self.count)
                self.pair_act(self.landed, which, s, p, ref)

    def run(self, use):
        if self.levels >= 2:
            self.relay_z()
        use(self.starts(0), self.block)
        if self.levels >= 1:
            self.await_pair(0)
            use(self.pair_starts(0), self.block)
        self.arrive_stage(0)
        self.arrive_stage(1)
        for s in (1, 2):
            use(self.starts(s), self.block)
        if self.levels >= 1:
            for s in (1, 2):
                self.await_pair(s)
                use(self.pair_starts(s), self.block)
        if self.levels >= 1:
            self.arrive_stage(2)
            use(self.starts(3), self.block)
            self.await_pair(3)
            use(self.pair_starts(3), self.block)
        else:
            for index in range(self.sub):
                for link in (1, 0):
                    self.arrive(0, link, 2, index)
                    p = (0 if link else 1) * self.sub + index
                    use([self.start_of(self.units[0], 3) + p * self.count], self.count)
        self.finish()


class Reduce(Sender):
    def __init__(self, at, levels, term, near, stage, row_buf, z_buf, sems):
        super().__init__()
        self.at, self.levels, self.term = at, levels, term
        self.halves = 2 ** (levels - 1)
        self.block = term.shape[0] // (8 * self.halves)
        self.near_buf, self.stage_buf, self.row_buf, self.z_buf = near, stage, row_buf, z_buf
        self.pair_send, self.pair_recv, self.row_send, self.row_recv, self.z_send, self.z_recv = sems

    def start_of(self, half, core, s):
        return ((half * 2 + core) * 4 + self.at.ring[s]) * self.block

    def own(self, half, s):
        return rows_at(self.term, self.start_of(half, self.at.core, s), self.block)

    def near(self, half, s):
        return self.near_buf.at[pl.ds((half * 4 + s) * self.block, self.block)]

    def stage(self, half, s):
        return self.stage_buf.at[pl.ds((half * 4 + s) * self.block, self.block)]

    def arrived(self, half, k):
        rows = self.block // 2
        return self.row_buf.at[pl.ds((half * 6 + k) * rows, rows)]

    def landed(self, dst, send, recv, peer):
        push(dst, dst, send, recv, peer).wait_recv()

    def produce(self, s, place):
        halves, core = range(self.halves), self.at.core
        away = [self.start_of(half, 1 - core, s) for half in halves]
        place(away, self.block)
        for half in halves:
            self.go(
                rows_at(self.term, away[half], self.block),
                self.near(half, s),
                self.pair_send.at[half, s],
                self.pair_recv.at[half, s],
                self.at.partner,
            )
        place([self.start_of(half, core, s) for half in halves], self.block)

    def await_pair(self, s):
        for half in range(self.halves):
            self.landed(self.near(half, s), self.pair_send.at[half, s], self.pair_recv.at[half, s], self.at.partner)

    def row_copy(self, half, k, src):
        peer = self.at.side if k in (0, 1, 5) else self.at.over
        self.go(src, self.arrived(half, k), self.row_send.at[half, k], self.row_recv.at[half, k], peer)

    def await_row(self, half, k):
        peer = self.at.side if k in (0, 1, 5) else self.at.over
        self.landed(self.arrived(half, k), self.row_send.at[half, k], self.row_recv.at[half, k], peer)

    def add_half(self, half, s, part, k, extra):
        out = half_of(self.stage(half, s), part)
        add_all(out, [half_of(self.own(half, s), part), half_of(self.near(half, s), part)] + extra)
        self.row_copy(half, k, out)

    def run(self, place, panel, dst):
        halves = range(self.halves)
        self.produce(3, place)
        self.produce(1, place)
        self.await_pair(3)
        for half in halves:
            self.add_half(half, 3, 0, 0, [])
            self.add_half(half, 3, 1, 3, [])
        self.produce(2, place)
        self.await_pair(1)
        for half in halves:
            self.add_half(half, 1, 0, 1, [])
        self.await_pair(2)
        for half in halves:
            self.add_half(half, 2, 1, 4, [])
        self.produce(0, place)
        for half in halves:
            self.await_row(half, 0)
            self.add_half(half, 2, 0, 2, [self.arrived(half, 0)])
            self.await_row(half, 3)
            self.add_half(half, 1, 1, 5, [self.arrived(half, 3)])
        self.await_pair(0)
        for half in halves:
            for k in (1, 4, 2, 5):
                self.await_row(half, k)

        def finish(out, half, extra, base):
            for part in range(2):
                terms = [half_of(self.own(half, 0), part), half_of(self.near(half, 0), part)]
                terms += [self.arrived(half, 1 + 3 * part), self.arrived(half, 2 + 3 * part)]
                terms += [half_of(ref, part) for ref in extra]
                add_all(half_of(out, part), terms, None if base is None else half_of(base, part))

        def finish_dynamic(out, half, extra, base):
            size, rows = self.block, self.block // 2
            own = rows_at(self.term, self.start_of(half, self.at.core, 0), size)
            near = rows_at(self.near_buf, half * 4 * size, size)
            for part in range(2):
                terms = [half_of(own, part), half_of(near, part)]
                for k in (1 + 3 * part, 2 + 3 * part):
                    terms.append(rows_at(self.row_buf, (half * 6 + k) * rows, rows))
                terms += [half_of(ref, part) for ref in extra]
                add_all(half_of(out, part), terms, None if base is None else half_of(base, part))

        if self.levels == 1:
            finish(dst, 0, [], panel)
        else:
            mine, theirs = half_of(self.z_buf, 0), half_of(self.z_buf, 1)
            finish_dynamic(mine, 1 - self.at.upper, [], None)
            self.go(mine, theirs, self.z_send.at[0], self.z_recv.at[0], self.at.across)
            self.landed(theirs, self.z_send.at[0], self.z_recv.at[0], self.at.across)
            finish_dynamic(dst, self.at.upper, [theirs], panel)
        self.finish()


def panel_kernel(
    low_hbm, mid_hbm, top_hbm, inv_low_hbm, inv_mid_hbm, inv_top_hbm, cpl_low_hbm, cpl_mid_hbm,
    parents_low, parents_mid,
    out_low, out_mid, out_top,
    inv_low, inv_mid, inv_top, cpl_low, cpl_mid, panel_mid, panel_top,
    buf_a, buf_b, buf_c, buf_t, near, stage, row_buf, z_buf, cast_low, part, picked, wide,
    load, *sems,
):
    at = Place(4, 2)
    pulls = {}
    order = [
        ("low", low_hbm, rows_at(buf_a, at.row * low_hbm.shape[0], low_hbm.shape[0])),
        ("inv_low", inv_low_hbm, inv_low),
        ("cpl_low", cpl_low_hbm, cpl_low),
        ("panel_mid", mid_hbm, panel_mid),
        ("inv_mid", inv_mid_hbm, inv_mid),
        ("cpl_mid", cpl_mid_hbm, cpl_mid),
        ("panel_top", top_hbm, panel_top),
        ("inv_top", inv_top_hbm, inv_top),
    ]
    for index, (name, src, dst) in enumerate(order):
        pulls[name] = pltpu.make_async_copy(src, dst, load.at[index])

    def need(*names):
        for name in names:
            pulls.pop(name).wait()

    pulls["low"].start()
    at.greet()
    low_sems, mid_sems, mid_sems2, top_sems, top_sems2, low_red, top_red = (
        sems[0:6], sems[6:12], sems[12:18], sems[18:24], sems[24:30], sems[30:36], sems[36:42]
    )
    low = Exchange(at, buf_a, 0, 2, low_sems, low_hbm)
    for p in (0, 2, 1, 3):
        low.send_piece(0, p)
    for name in list(pulls)[1:]:
        pulls[name].start()
    low_targets = parents_low[pl.ds(at.group, 1), :]
    mid_targets = parents_mid[pl.ds(at.group // 2, 1), :]
    spread_lanes(wide, mid_targets)
    need("low", "inv_low")

    def user(matrix, panel, total, sign):
        first = [sign > 0]

        def use(starts, depth):
            for start in starts:
                multiply(matrix, panel, total, start, depth, sign, first[0])
                first[0] = False

        return use

    def picker(panel):
        first = [True]

        def use(starts, depth):
            pick_add(picked, wide, panel, starts, depth, first[0])
            first[0] = False

        return use

    low.run(user(inv_low, buf_a, out_low, 1))

    cast_low[...] = out_low[...].astype(jnp.bfloat16)
    need("cpl_low")
    couple_rows(cpl_low, cast_low[...], part)
    mid = Exchange(at, buf_b, 1, 1, mid_sems)
    reduce_mid = Reduce(at, 1, buf_t, near, stage, row_buf, z_buf, low_red)
    need("panel_mid")
    own = rows_at(buf_b, mid.mine, mid.block)
    reduce_mid.run(lambda starts, count: place_rows(buf_t, part, low_targets, starts, count), panel_mid, own)
    for p in range(2):
        mid.send_piece(0, p)
    need("inv_mid")
    mid.run(user(inv_mid, buf_b, out_mid, 1))

    need("cpl_mid")
    couple_rows(cpl_mid, out_mid[...].astype(jnp.bfloat16), part)
    top = Exchange(at, buf_c, 2, 1, top_sems)
    reduce_top = Reduce(at, 2, buf_t, near, stage, row_buf, z_buf, top_red)
    need("panel_top")
    own = rows_at(buf_c, top.mine, top.block)
    reduce_top.run(lambda starts, count: place_rows(buf_t, part, mid_targets, starts, count), panel_top, own)
    for p in range(2):
        top.send_piece(0, p)
    need("inv_top")
    top.run(user(inv_top, buf_c, out_top, 1))

    back = Exchange(at, buf_t, 2, 1, top_sems2)
    rows_at(buf_t, back.mine, back.block)[...] = out_top[...].astype(jnp.bfloat16)
    for p in range(2):
        back.send_piece(0, p)
    back.run(picker(buf_t))

    part[...] = picked[...].astype(jnp.bfloat16)
    lift = Exchange(at, buf_b, 1, 1, mid_sems)
    for p in range(2):
        rows_at(buf_b, lift.mine + p * lift.count, lift.count)[...] = lift_rows(
            cpl_mid, part[...], p * lift.count, lift.count
        ).astype(jnp.bfloat16)
        lift.send_piece(0, p)
    spread_lanes(wide, low_targets)
    lift.run(user(inv_mid, buf_b, out_mid, -1))

    back = Exchange(at, buf_c, 1, 1, mid_sems2)
    rows_at(buf_c, back.mine, back.block)[...] = out_mid[...].astype(jnp.bfloat16)
    for p in range(2):
        back.send_piece(0, p)
    back.run(picker(buf_c))

    part[...] = picked[...].astype(jnp.bfloat16)
    lift = Exchange(at, buf_a, 0, 2, low_sems)
    for p in (0, 2, 1, 3):
        rows_at(buf_a, lift.mine + p * lift.count, lift.count)[...] = lift_rows(
            cpl_low, part[...], p * lift.count, lift.count
        ).astype(jnp.bfloat16)
        lift.send_piece(0, p)
    lift.run(user(inv_low, buf_a, out_low, -1))


def gather_sems(levels, sub):
    units = 2 if levels >= 2 else 1
    rows, pairs = units * 6 * sub, 4 * 2 * sub
    return [dma(units, 6 * sub)] * 2 + [dma(units, pairs)] * 2 + [dma(2), dma(2)]


def reduce_sems(levels):
    halves = 2 ** (levels - 1)
    return [dma(halves, 4)] * 2 + [dma(halves, 6)] * 2 + [dma(1), dma(1)]


def solve_panel(
    panel_low, panel_mid, panel_top, inverse_low, inverse_mid, inverse_top, couple_low, couple_mid,
    parents_low, parents_mid,
):
    width = panel_low.shape[1]
    front, links = inverse_low.shape[2], couple_low.shape[1]

    def vmem(*shape, kind=jnp.bfloat16):
        return pltpu.VMEM(shape, kind)

    scratch = [vmem(*m.shape) for m in (inverse_low, inverse_mid, inverse_top, couple_low, couple_mid)]
    scratch += [vmem(*panel_mid.shape), vmem(*panel_top.shape)]
    scratch += [vmem(front, width)] * 4
    scratch += [vmem(front // 2, width)] * 2 + [vmem(front * 3 // 8, width), vmem(2 * panel_top.shape[0], width)]
    scratch += [vmem(*panel_low.shape), vmem(links, width), vmem(links, width, kind=jnp.float32)]
    scratch += [vmem(links, 128, kind=jnp.int32), dma(8)]
    scratch += gather_sems(0, 2) + gather_sems(1, 1) * 2 + gather_sems(2, 1) * 2
    scratch += reduce_sems(1) + reduce_sems(2)
    return pl.pallas_call(
        panel_kernel,
        out_shape=tuple(
            jax.ShapeDtypeStruct(p.shape, jnp.float32) for p in (panel_low, panel_mid, panel_top)
        ),
        in_specs=[HBM_SPEC] * 8 + [VMEM_SPEC] * 2,
        out_specs=(VMEM_SPEC,) * 3,
        scratch_shapes=scratch,
        compiler_params=params(7, 63),
    )(
        panel_low, panel_mid, panel_top, inverse_low, inverse_mid, inverse_top, couple_low, couple_mid,
        parents_low, parents_mid,
    )


def on_device(
    n,
    panel_low,
    panel_mid,
    panel_top,
    inverse_low,
    inverse_mid,
    inverse_top,
    couple_low,
    couple_mid,
    parents_low,
    parents_mid,
):
    if n == 4:
        return solve_panel(
            panel_low, panel_mid, panel_top, inverse_low, inverse_mid, inverse_top, couple_low, couple_mid,
            parents_low, parents_mid,
        )
    group = lax.axis_index("grp")
    low_targets = lax.dynamic_index_in_dim(parents_low, group, 0, keepdims=False)
    mid_targets = lax.dynamic_index_in_dim(parents_mid, group // 2, 0, keepdims=False)
    low_y = gather_solve(panel_low, inverse_low, n, 0, 0)
    term = spread_rows(complex_product(couple_low, low_y.astype(jnp.bfloat16)), low_targets)
    mid_y = reduce_solve(term, panel_mid, inverse_mid, n, 1, 1)
    term = spread_rows(complex_product(couple_mid, mid_y.astype(jnp.bfloat16)), mid_targets)
    top_x = reduce_solve(term, panel_top, inverse_top, n, 2, 2)
    top_full = gather(top_x.astype(jnp.bfloat16), n, 2, 3)
    lift = transposed_product(couple_mid, pick_rows(top_full, mid_targets)).astype(jnp.bfloat16)
    mid_x = mid_y - gather_solve(lift, inverse_mid, n, 1, 4)
    mid_full = gather(mid_x.astype(jnp.bfloat16), n, 1, 5)
    lift = transposed_product(couple_low, pick_rows(mid_full, low_targets)).astype(jnp.bfloat16)
    low_x = low_y - gather_solve(lift, inverse_low, n, 0, 6)
    return (low_x, mid_x, top_x)


def solution(mesh):
    placed = (
        P(("grp", "row"), None),
        P(("grp", "row"), None),
        P(("grp", "row"), None),
        P(None, ("grp", "row"), None),
        P(None, ("grp", "row"), None),
        P(None, ("grp", "row"), None),
        P(None, None, ("grp", "row")),
        P(None, None, ("grp", "row")),
        P(),
        P(),
    )
    return jax.shard_map(
        functools.partial(on_device, mesh.shape["row"]),
        mesh=mesh,
        in_specs=placed,
        out_specs=(P(("grp", "row"), None), P(("grp", "row"), None), P(("grp", "row"), None)),
        check_vma=False,
    )
```

```python
import functools
import math

import jax
import jax.numpy as jnp
from jax import lax
from jax.experimental import pallas as pl
from jax.experimental.pallas import tpu as pltpu
from jax.sharding import PartitionSpec as P

F = 4096
MESH = pl.DeviceIdType.MESH


def complex_product(matrix, panel):
    width = panel.shape[1] // 2
    real_term = jnp.dot(matrix[0], panel, preferred_element_type=jnp.float32)
    imag_term = jnp.dot(matrix[1], panel, preferred_element_type=jnp.float32)
    return real_term + jnp.concatenate([-imag_term[:, width:], imag_term[:, :width]], axis=1)


def transposed_product(matrix, panel):
    width = panel.shape[1] // 2
    contract = (((0,), (0,)), ((), ()))
    real_term = lax.dot_general(matrix[0], panel, contract, preferred_element_type=jnp.float32)
    imag_term = lax.dot_general(matrix[1], panel, contract, preferred_element_type=jnp.float32)
    return real_term + jnp.concatenate([-imag_term[:, width:], imag_term[:, :width]], axis=1)


class Place:
    def __init__(self, n, levels):
        self.n = n
        self.levels = levels
        self.square = n == 4
        self.group = lax.axis_index("grp")
        self.row = lax.axis_index("row")
        self.core = lax.rem(self.group, 2)
        self.upper = lax.rem(self.group // 2, 2)
        self.partner = (self.group + 1 - 2 * self.core, self.row)
        self.across = (self.group + 2 - 4 * self.upper, self.row)
        self.unit = lax.rem(self.group, 2**levels)
        if self.square:
            side = self.row + 1 - 2 * lax.rem(self.row, 2)
            over = self.row + 2 - 4 * (self.row // 2)
            self.ring = [self.row, side, over, 3 - self.row]
            self.side = (self.group, side)
            self.over = (self.group, over)

    def ahead(self, step):
        return self.ring[step] if self.square else lax.rem(self.row + step, self.n)

    def behind(self, step):
        return self.ring[step] if self.square else lax.rem(self.row + self.n - step, self.n)

    def greet(self):
        barrier = pltpu.get_barrier_semaphore()
        if self.square:
            peers = [self.side, self.over]
        else:
            peers = [(self.group, self.ahead(s)) for s in range(1, self.n)]
        if self.levels >= 1:
            peers.append(self.partner)
        if self.levels >= 2:
            peers.append(self.across)
        for peer in peers:
            pl.semaphore_signal(barrier, inc=1, device_id=peer, device_id_type=MESH)
        pl.semaphore_wait(barrier, len(peers))


def push(src, dst, send, recv, peer):
    return pltpu.make_async_remote_copy(
        src_ref=src, dst_ref=dst, send_sem=send, recv_sem=recv, device_id=peer, device_id_type=MESH
    )


def half_of(ref, index):
    rows = ref.shape[0] // 2
    return ref.at[pl.ds(index * rows, rows)]


def spread(at, out, sems, use):
    n, levels = at.n, at.levels
    row_send, row_recv, pair_send, pair_recv, z_send, z_recv = sems
    near = at.unit
    started = []

    def go(src, send, recv, peer):
        copy = push(src, src, send, recv, peer)
        copy.start()
        started.append(copy)

    def landed(ref, send, recv, peer):
        push(ref, ref, send, recv, peer).wait_recv()

    def row_copy(act, which, k, slot, half, peer):
        act(half_of(out.at[slot], half), row_send.at[which, k], row_recv.at[which, k], peer)

    def to_rows(which, unit):
        mine = unit * n + at.row
        if at.square:
            row_copy(go, which, 0, mine, 0, at.side)
            row_copy(go, which, 1, mine, 1, at.over)
            row_copy(go, which, 2, mine, 1, at.side)
            row_copy(go, which, 3, mine, 0, at.over)
            return
        for s in range(1, n):
            go(out.at[mine], row_send.at[which, s], row_recv.at[which, s], (at.group, at.ahead(s)))

    def forward(which, unit):
        if at.square:
            side, over = unit * n + at.ring[1], unit * n + at.ring[2]
            row_copy(landed, which, 0, side, 0, at.side)
            row_copy(go, which, 4, side, 0, at.over)
            row_copy(landed, which, 1, over, 1, at.over)
            row_copy(go, which, 5, over, 1, at.side)

    def await_row(which, unit, s):
        slot = unit * n + at.behind(s)
        if not at.square:
            peer = (at.group, at.behind(s))
            landed(out.at[slot], row_send.at[which, s], row_recv.at[which, s], peer)
        elif s == 1:
            row_copy(landed, which, 2, slot, 1, at.side)
        elif s == 2:
            row_copy(landed, which, 3, slot, 0, at.over)
        else:
            row_copy(landed, which, 4, slot, 0, at.over)
            row_copy(landed, which, 5, slot, 1, at.side)

    def to_pair(which, s, unit):
        src = out.at[unit * n + at.behind(s)]
        go(src, pair_send.at[which, s], pair_recv.at[which, s], at.partner)

    def await_pair(which, s, unit):
        slot = (unit + 1 - 2 * at.core) * n + at.behind(s)
        landed(out.at[slot], pair_send.at[which, s], pair_recv.at[which, s], at.partner)
        use(slot)

    units = [near]
    if levels >= 2:
        units.append(lax.rem(near + 2, 4))
        go(out.at[near * n + at.row], z_send.at[0], z_recv.at[0], at.across)
    to_rows(0, near)
    if levels >= 1:
        to_pair(0, 0, near)
    if levels >= 2:
        landed(out.at[units[1] * n + at.row], z_send.at[0], z_recv.at[0], at.across)
        to_rows(1, units[1])
        to_pair(1, 0, units[1])
    use(near * n + at.row)
    if levels >= 2:
        use(units[1] * n + at.row)
    for which, unit in enumerate(units):
        forward(which, unit)
    for s in range(1, n):
        for which, unit in enumerate(units):
            await_row(which, unit, s)
            if levels >= 1:
                to_pair(which, s, unit)
                await_pair(which, s - 1, unit)
            use(unit * n + at.behind(s))
    if levels >= 1:
        for which, unit in enumerate(units):
            await_pair(which, n - 1, unit)
    for copy in started:
        copy.wait_send()


def solver(n, out, inverse_hbm, inverse, turned, total, sem):
    count, block, width = out.shape
    rows = inverse.shape[1]
    tile = min(rows, 256)
    whole = block % 128 == 0
    together = 1 if whole else turned.shape[0] // block
    copy = pltpu.make_async_copy(inverse_hbm, inverse, sem)
    copy.start()
    waiting = [copy]

    def multiply(slot, first):
        panel = out[slot] if whole else out[pl.ds(slot, together)].reshape(turned.shape)
        half = width // 2
        turned[:, :half] = -panel[:, half:]
        turned[:, half:] = panel[:, :half]
        span_columns = turned.shape[0]
        columns = pl.ds(pl.multiple_of(slot // together * span_columns, span_columns), span_columns)

        def body(index, carry):
            span = pl.ds(pl.multiple_of(index * tile, tile), tile)
            block_now = out[slot] if whole else panel
            real = jnp.dot(inverse[0, span, columns], block_now, preferred_element_type=jnp.float32)
            imag = jnp.dot(inverse[1, span, columns], turned[...], preferred_element_type=jnp.float32)
            if first:
                total[span, :] = real + imag
            else:
                total[span, :] = total[span, :] + (real + imag)
            return carry

        lax.fori_loop(0, rows // tile, body, 0)

    def use(slot):
        if whole:
            first = bool(waiting)
            if first:
                waiting.pop().wait()
            multiply(slot, first)

    def rest():
        if not whole:
            waiting.pop().wait()
            for slot in range(0, count, together):
                multiply(slot, slot == 0)

    return use, rest


def gather_kernel(n, levels, own, full, *sems):
    at = Place(n, levels)
    at.greet()
    full[at.unit * n + at.row] = own[...]
    spread(at, full, sems, lambda slot: None)


def gather_solve_kernel(n, levels, own, inverse_hbm, total, full, inverse, turned, sem, *sems):
    at = Place(n, levels)
    use, rest = solver(n, full, inverse_hbm, inverse, turned, total, sem)
    at.greet()
    full[at.unit * n + at.row] = own[...]
    spread(at, full, sems, use)
    rest()


def add_rows(out_ref, terms, panel=None):
    rows = out_ref.shape[0]
    step = min(rows, 64)

    def body(index, carry):
        span = pl.ds(pl.multiple_of(index * step, step), step)
        total = terms[0][span, :].astype(jnp.float32)
        for term in terms[1:]:
            total = total + term[span, :].astype(jnp.float32)
        if panel is not None:
            total = panel[span, :].astype(jnp.float32) - total
        out_ref[span, :] = total.astype(out_ref.dtype)
        return carry

    lax.fori_loop(0, rows // step, body, 0)


def reduce_solve_kernel(
    n, levels, term, panel, inverse_hbm, total, full, inverse, turned, near_buf, stage, row_buf, z_buf, sem, *sems
):
    at = Place(n, levels)
    halves = 2 ** (levels - 1)
    spread_sems = sems[:6]
    pair_send, pair_recv, row_send, row_recv, z_send, z_recv = sems[6:]
    use, finish_solve = solver(n, full, inverse_hbm, inverse, turned, total, sem)
    at.greet()
    started = []

    def go(src, dst, send, recv, peer):
        copy = push(src, dst, send, recv, peer)
        copy.start()
        started.append(copy)

    def landed(ref, send, recv, peer):
        push(ref, ref, send, recv, peer).wait_recv()

    order = [3, 1, 2, 0] if at.square else list(range(1, n)) + [0]
    for s in order:
        for half in range(halves):
            src = term.at[(half * 2 + 1 - at.core) * n + at.ahead(s)]
            go(src, near_buf.at[half, s], pair_send.at[half, s], pair_recv.at[half, s], at.partner)

    def own_term(half, s):
        return term.at[(half * 2 + at.core) * n + at.ahead(s)]

    def await_pair(half, s):
        landed(near_buf.at[half, s], pair_send.at[half, s], pair_recv.at[half, s], at.partner)

    def row_copy(half, k, src, peer):
        go(src, row_buf.at[half, k], row_send.at[half, k], row_recv.at[half, k], peer)

    def await_row(half, k, peer):
        landed(row_buf.at[half, k], row_send.at[half, k], row_recv.at[half, k], peer)

    if at.square:
        for half in range(halves):
            await_pair(half, 3)
            add_rows(stage.at[half, 3], [own_term(half, 3), near_buf.at[half, 3]])
            row_copy(half, 0, half_of(stage.at[half, 3], 0), at.side)
            row_copy(half, 3, half_of(stage.at[half, 3], 1), at.over)
        for half in range(halves):
            await_pair(half, 1)
            first = half_of(stage.at[half, 1], 0)
            add_rows(first, [half_of(own_term(half, 1), 0), half_of(near_buf.at[half, 1], 0)])
            row_copy(half, 1, first, at.side)
            await_pair(half, 2)
            second = half_of(stage.at[half, 2], 1)
            add_rows(second, [half_of(own_term(half, 2), 1), half_of(near_buf.at[half, 2], 1)])
            row_copy(half, 4, second, at.over)
        for half in range(halves):
            await_row(half, 0, at.side)
            first = half_of(stage.at[half, 2], 0)
            near = half_of(near_buf.at[half, 2], 0)
            add_rows(first, [half_of(own_term(half, 2), 0), near, row_buf.at[half, 0]])
            row_copy(half, 2, first, at.over)
            await_row(half, 3, at.over)
            second = half_of(stage.at[half, 1], 1)
            near = half_of(near_buf.at[half, 1], 1)
            add_rows(second, [half_of(own_term(half, 1), 1), near, row_buf.at[half, 3]])
            row_copy(half, 5, second, at.side)
        for half in range(halves):
            await_pair(half, 0)
            await_row(half, 1, at.side)
            await_row(half, 4, at.over)
            await_row(half, 2, at.over)
            await_row(half, 5, at.side)
    else:
        for s in range(1, n):
            for half in range(halves):
                await_pair(half, s)
                add_rows(stage.at[half, s], [own_term(half, s), near_buf.at[half, s]])
                row_copy(half, s, stage.at[half, s], (at.group, at.ahead(s)))
        for half in range(halves):
            await_pair(half, 0)
            for s in range(1, n):
                await_row(half, s, (at.group, at.behind(s)))

    def finish(dst, half, extra, base):
        own, near = own_term(half, 0), near_buf.at[half, 0]
        if not at.square:
            rest = [row_buf.at[half, s] for s in range(1, n)]
            add_rows(dst, [own, near] + rest + extra, base)
            return
        for part in range(2):
            rest = [row_buf.at[half, 1 + 3 * part], row_buf.at[half, 2 + 3 * part]]
            rest = rest + [half_of(ref, part) for ref in extra]
            terms = [half_of(own, part), half_of(near, part)] + rest
            add_rows(half_of(dst, part), terms, None if base is None else half_of(base, part))

    slot = at.unit * n + at.row
    if levels == 1:
        finish(full.at[slot], 0, [], panel)
    else:
        finish(z_buf.at[0], 1 - at.upper, [], None)
        go(z_buf.at[0], z_buf.at[1], z_send.at[0], z_recv.at[0], at.across)
        landed(z_buf.at[1], z_send.at[0], z_recv.at[0], at.across)
        finish(full.at[slot], at.upper, [z_buf.at[1]], panel)
    spread(at, full, spread_sems, use)
    finish_solve()
    for copy in started:
        copy.wait_send()


def dma(*shape):
    return pltpu.SemaphoreType.DMA(shape)


VMEM_SPEC = pl.BlockSpec(memory_space=pltpu.VMEM)
HBM_SPEC = pl.BlockSpec(memory_space=pltpu.HBM)


def spread_scratch(n):
    k = max(n, 6)
    return [dma(2, k), dma(2, k), dma(2, n), dma(2, n), dma(1), dma(1)]


def params(ident, mebibytes):
    return pltpu.CompilerParams(
        collective_id=ident, has_side_effects=True, vmem_limit_bytes=mebibytes << 20
    )


def gather(own, n, levels, ident):
    block, width = own.shape
    count = 2**levels * n
    full = pl.pallas_call(
        functools.partial(gather_kernel, n, levels),
        out_shape=jax.ShapeDtypeStruct((count, block, width), own.dtype),
        in_specs=[VMEM_SPEC],
        out_specs=VMEM_SPEC,
        scratch_shapes=spread_scratch(n),
        compiler_params=params(ident, 16),
    )(own)
    return full.reshape(count * block, width)


def solve_scratch(inverse, block, width, count):
    return [
        pltpu.VMEM((count, block, width), jnp.bfloat16),
        pltpu.VMEM(inverse.shape, inverse.dtype),
        pltpu.VMEM((block if block % 128 == 0 else 512, width), jnp.bfloat16),
    ]


def gather_solve(own, inverse, n, levels, ident):
    block, width = own.shape
    return pl.pallas_call(
        functools.partial(gather_solve_kernel, n, levels),
        out_shape=jax.ShapeDtypeStruct((inverse.shape[1], width), jnp.float32),
        in_specs=[VMEM_SPEC, HBM_SPEC],
        out_specs=VMEM_SPEC,
        scratch_shapes=solve_scratch(inverse, block, width, 2**levels * n)
        + [pltpu.SemaphoreType.DMA]
        + spread_scratch(n),
        compiler_params=params(ident, 32),
    )(own, inverse)


def reduce_solve(term, panel, inverse, n, levels, ident):
    block, width = panel.shape
    count = 2**levels * n
    halves = 2 ** (levels - 1)
    whole = pltpu.VMEM((halves, n, block, width), jnp.bfloat16)
    if n == 4:
        pieces, k = pltpu.VMEM((halves, 6, block // 2, width), jnp.bfloat16), 6
    else:
        pieces, k = whole, n
    return pl.pallas_call(
        functools.partial(reduce_solve_kernel, n, levels),
        out_shape=jax.ShapeDtypeStruct((inverse.shape[1], width), jnp.float32),
        in_specs=[VMEM_SPEC, VMEM_SPEC, HBM_SPEC],
        out_specs=VMEM_SPEC,
        scratch_shapes=solve_scratch(inverse, block, width, count)
        + [whole, whole, pieces, pltpu.VMEM((2, block, width), jnp.bfloat16)]
        + [pltpu.SemaphoreType.DMA]
        + spread_scratch(n)
        + [dma(halves, n), dma(halves, n), dma(halves, k), dma(halves, k), dma(1), dma(1)],
        compiler_params=params(ident, 32),
    )(term.reshape(count, block, width), panel, inverse)


def spread_kernel(tile, targets, rows, out):
    index = lax.broadcasted_iota(jnp.int32, (tile, 1), 0) + pl.program_id(0) * tile
    marks = (index == targets[...]).astype(jnp.float32).astype(jnp.bfloat16)
    out[...] = jnp.dot(marks, rows[...], preferred_element_type=jnp.float32).astype(out.dtype)


def spread_rows(partial_rows, targets):
    count, width = partial_rows.shape
    tile = F // 4
    return pl.pallas_call(
        functools.partial(spread_kernel, tile),
        grid=(F // tile,),
        in_specs=[
            pl.BlockSpec((1, count), lambda i: (0, 0)),
            pl.BlockSpec((count, width), lambda i: (0, 0)),
        ],
        out_specs=pl.BlockSpec((tile, width), lambda i: (i, 0)),
        out_shape=jax.ShapeDtypeStruct((F, width), jnp.bfloat16),
        compiler_params=pltpu.CompilerParams(vmem_limit_bytes=32 << 20),
    )(targets[None, :], partial_rows.astype(jnp.bfloat16))


def pick_rows(panel, targets):
    marks = (targets[:, None] == lax.broadcasted_iota(jnp.int32, (1, F), 1)).astype(jnp.bfloat16)
    return jnp.dot(marks, panel, preferred_element_type=jnp.float32).astype(jnp.bfloat16)


def dot32(left, right):
    return jnp.dot(left, right, preferred_element_type=jnp.float32)


def turn(product):
    half, width = product.shape[0] // 2, product.shape[1] // 2
    real, imag = product[:half], product[half:]
    return real + jnp.concatenate([-imag[:, width:], imag[:, :width]], axis=1)


def rows_at(ref, start, count):
    return ref.at[pl.ds(pl.multiple_of(start, math.gcd(count, 256)), count)]


def multiply(matrix, panel, total, start, depth, sign):
    rows = matrix.shape[1]
    tile = min(rows, 512)
    span = pl.ds(pl.multiple_of(start, depth), depth)
    block = panel[span, :]
    for base in range(0, rows, tile):
        part = pl.ds(base, tile)
        left = matrix[:, part, span].reshape(2 * tile, depth)
        product = turn(dot32(left, block))
        total[part, :] = total[part, :] + product if sign > 0 else total[part, :] - product


def choose(index, values):
    out = values[-1]
    for k in range(len(values) - 2, -1, -1):
        out = jnp.where(index == k, values[k], out)
    return out


def stepped(count, before, step, after):
    def body(index, carry):
        for k, event in before.items():
            pl.when(index == k)(event)
        step(index)
        for k, event in after.items():
            pl.when(index == k)(event)
        return carry

    lax.fori_loop(0, count, body, 0)


def couple_rows(matrix, panel, out):
    tile = 1024
    for base in range(0, matrix.shape[1], tile):
        part = pl.ds(base, tile)
        left = matrix[:, part, :].reshape(2 * tile, matrix.shape[2])
        out[part, :] = turn(dot32(left, panel)).astype(out.dtype)


def lift_rows(matrix, panel, start, count):
    columns = pl.ds(start, count)
    contract = (((0,), (0,)), ((), ()))
    real = lax.dot_general(matrix[0, :, columns], panel, contract, preferred_element_type=jnp.float32)
    imag = lax.dot_general(matrix[1, :, columns], panel, contract, preferred_element_type=jnp.float32)
    width = panel.shape[1] // 2
    return real + jnp.concatenate([-imag[:, width:], imag[:, :width]], axis=1)


def place_rows(term, part, targets, starts, count):
    iota = lax.broadcasted_iota(jnp.int32, (count, 1), 0)
    marks = [(iota + start == targets).astype(jnp.float32).astype(jnp.bfloat16) for start in starts]
    placed = dot32(jnp.concatenate(marks, axis=0), part[...])
    for index, start in enumerate(starts):
        rows_at(term, start, count)[...] = placed[index * count : (index + 1) * count].astype(term.dtype)


def spread_lanes(wide, targets):
    for base in range(0, wide.shape[0], 128):
        square = jnp.broadcast_to(targets[:, base : base + 128], (128, 128))
        wide[pl.ds(base, 128), :] = square.T


def pick_add(total, wide, panel, starts, depth):
    blocks = [panel[pl.ds(pl.multiple_of(start, depth), depth), :] for start in starts]
    block = jnp.concatenate(blocks, axis=0) if len(blocks) > 1 else blocks[0]
    lanes = lax.broadcasted_iota(jnp.int32, (1, 128), 1)
    tile = 1024
    for base in range(0, wide.shape[0], tile):
        part = pl.ds(base, tile)
        wanted = wide[part, :]
        marks = []
        for start in starts:
            for shift in range(0, depth, 128):
                marks.append((lanes + (start + shift) == wanted).astype(jnp.float32).astype(jnp.bfloat16))
        total[part, :] = total[part, :] + dot32(jnp.concatenate(marks, axis=1), block)


def add_all(out, terms, base=None):
    total = terms[0][...].astype(jnp.float32)
    for term in terms[1:]:
        total = total + term[...].astype(jnp.float32)
    if base is not None:
        total = base[...].astype(jnp.float32) - total
    out[...] = total.astype(out.dtype)


class Sender:
    def __init__(self):
        self.log = {}

    def send(self, key):
        self.copy(*key).start()
        self.log[key] = True

    def land(self, key):
        self.copy(*key, arriving=True).wait_recv()

    def sent(self, *keys):
        for key in keys:
            del self.log[key]
            self.copy(*key).wait_send()

    def finish(self):
        self.sent(*list(self.log))


class Exchange(Sender):
    def __init__(self, at, buf, levels, sems, source=None):
        super().__init__()
        self.at, self.buf, self.levels, self.sems, self.source = at, buf, levels, sems, source
        self.block = buf.shape[0] // (4 * 2**levels)
        self.sub = 2 if levels == 0 else 1
        self.count = self.block // (2 * self.sub)
        near = lax.rem(at.group, 2**levels)
        self.units = [near]
        if levels >= 2:
            self.units.append(lax.rem(near + 2, 4))
        self.mine = self.start_of(near, 0)

    def start_of(self, unit, s):
        return (unit * 4 + self.at.ring[s]) * self.block

    def copy(self, kind, which, a, b, arriving=False):
        row_send, row_recv, pair_send, pair_recv, z_send, z_recv = self.sems
        at, unit, index = self.at, self.units[which], 0
        if kind == "row":
            link, stage, index = a, b // self.sub, b % self.sub
            outward = [(0, link), (0, 1 - link), (2 - link, 1 - link)]
            inward = [(1 + link, link), (1 + link, 1 - link), (3, 1 - link)]
            s, half = (inward if arriving else outward)[stage]
            k, peer = link * 3 * self.sub + b, at.over if link else at.side
            send, recv = row_send.at[which, k], row_recv.at[which, k]
        elif kind == "pair":
            s, half = a, b
            send, recv, peer = pair_send.at[which, 2 * s + half], pair_recv.at[which, 2 * s + half], at.partner
            unit = unit + 1 - 2 * at.core if arriving else unit
        else:
            s, half = 0, b
            send, recv, peer = z_send.at[half], z_recv.at[half], at.across
            unit = self.units[1] if arriving else self.units[0]
        shift = (half * self.sub + index) * self.count
        ref = rows_at(self.buf, self.start_of(unit, s) + shift, self.count)
        src = ref
        if self.source is not None and s == 0 and not arriving:
            src = self.source.at[pl.ds(shift, self.count)]
        return push(src, ref, send, recv, peer)

    def pieces(self):
        return [(half, index) for index in range(self.sub) for half in range(2)]

    def begin(self, half, index=0):
        self.send(("row", 0, half, index))
        if self.levels >= 2:
            self.send(("z", 0, 0, half))
        if self.levels >= 1:
            self.send(("pair", 0, 0, half))

    def arrive(self, which, link, stage, index=0):
        self.land(("row", which, link, stage * self.sub + index))
        if stage == 0:
            self.send(("row", which, 1 - link, 2 * self.sub + index))
        if self.levels >= 1:
            s, half = [(1 + link, link), (1 + link, 1 - link), (3, 1 - link)][stage]
            self.send(("pair", which, s, half))

    def both(self, which, stage):
        for link, index in self.pieces():
            self.arrive(which, link, stage, index)

    def second(self, which):
        for link, index in self.pieces():
            self.sent(("row", which, link, index))
            self.send(("row", which, link, self.sub + index))

    def await_pair(self, which, *rows):
        for s in rows:
            for half in range(2):
                self.land(("pair", which, s, half))

    def z_first(self):
        for half in range(2):
            self.land(("z", 0, 0, half))
            self.send(("row", 1, half, 0))
            self.send(("pair", 1, 0, half))

    def run(self, use):
        def block(which, other, s):
            return self.start_of(self.units[which] + (1 - 2 * self.at.core) * other, s)

        def then(*events):
            def event():
                for call, *arguments in events:
                    call(*arguments)

            return event

        if self.levels == 0:
            order = [(0, 0), (0, 1), (0, 2), (0, 3), (1, 0), (2, 2), (1, 1), (2, 3)]
            order += [(1, 2), (2, 0), (1, 3), (2, 1), (3, 0), (3, 2), (3, 1), (3, 3)]
            starts = [[block(0, 0, s) + piece * self.count for s, piece in order]]
            depth = self.count
            before = {4: then((self.second, 0), (self.both, 0, 0)), 8: then((self.both, 0, 1))}
            for step, (link, index) in ((12, (1, 0)), (13, (0, 0)), (14, (1, 1)), (15, (0, 1))):
                before[step] = then((self.arrive, 0, link, 2, index))
        elif self.levels == 1:
            order = [(0, 0), (1, 0), (0, 1), (0, 2), (1, 1), (1, 2), (0, 3), (1, 3)]
            starts = [[block(0, other, s) for other, s in order]]
            depth = self.block
            before = {
                1: then((self.second, 0), (self.await_pair, 0, 0)),
                2: then((self.both, 0, 0), (self.both, 0, 1)),
                4: then((self.await_pair, 0, 1)),
                5: then((self.await_pair, 0, 2)),
                6: then((self.both, 0, 2)),
                7: then((self.await_pair, 0, 3)),
            }
        else:
            starts = [
                [block(*b) for b in line]
                for line in (
                    [(0, 0, 0), (0, 0, 1), (1, 0, 0), (0, 1, 1), (0, 0, 3), (1, 0, 1), (1, 1, 1), (1, 0, 3)],
                    [(0, 1, 0), (0, 0, 2), (1, 1, 0), (0, 1, 2), (0, 1, 3), (1, 0, 2), (1, 1, 2), (1, 1, 3)],
                )
            ]
            depth = self.block
            before = {
                0: then((self.await_pair, 0, 0)),
                1: then((self.second, 0), (self.both, 0, 0), (self.z_first,), (self.both, 0, 1)),
                2: then((self.await_pair, 1, 0)),
                3: then((self.await_pair, 0, 1, 2)),
                4: then((self.second, 1), (self.both, 0, 2), (self.await_pair, 0, 3)),
                5: then((self.both, 1, 0), (self.both, 1, 1)),
                6: then((self.await_pair, 1, 1, 2)),
                7: then((self.both, 1, 2), (self.await_pair, 1, 3)),
            }
        count = len(starts[0])
        stepped(count, before, lambda i: use([choose(i, line) for line in starts], depth), {})
        self.finish()


class Reduce(Sender):
    def __init__(self, at, levels, term, near, stage, row_buf, z_buf, sems):
        super().__init__()
        self.at, self.levels, self.term, self.sems = at, levels, term, sems
        self.halves = 2 ** (levels - 1)
        self.block = term.shape[0] // (8 * self.halves)
        self.near_buf, self.stage_buf, self.row_buf, self.z_buf = near, stage, row_buf, z_buf

    def start_of(self, half, core, s):
        return ((half * 2 + core) * 4 + self.at.ring[s]) * self.block

    def own(self, half, s):
        return rows_at(self.term, self.start_of(half, self.at.core, s), self.block)

    def near(self, half, s):
        return rows_at(self.near_buf, (half * 4 + s) * self.block, self.block)

    def stage(self, half, s):
        return rows_at(self.stage_buf, (half * 4 + s) * self.block, self.block)

    def arrived(self, half, k):
        rows = self.block // 2
        return rows_at(self.row_buf, (half * 6 + k) * rows, rows)

    def copy(self, kind, half, k, arriving=False):
        pair_send, pair_recv, row_send, row_recv, z_send, z_recv = self.sems
        at = self.at
        if kind == "pair":
            away = rows_at(self.term, self.start_of(half, 1 - at.core, k), self.block)
            near = self.near(half, k)
            return push(near if arriving else away, near, pair_send.at[half, k], pair_recv.at[half, k], at.partner)
        if kind == "row":
            peer = at.side if k in (0, 1, 5) else at.over
            s, part = [(3, 0), (1, 0), (2, 0), (3, 1), (2, 1), (1, 1)][k]
            src = self.arrived(half, k) if arriving else half_of(self.stage(half, s), part)
            return push(src, self.arrived(half, k), row_send.at[half, k], row_recv.at[half, k], peer)
        mine, theirs = half_of(self.z_buf, 0), half_of(self.z_buf, 1)
        return push(theirs if arriving else mine, theirs, z_send.at[0], z_recv.at[0], at.across)

    def await_pair(self, s):
        for half in range(self.halves):
            self.land(("pair", half, s))

    def add_half(self, half, k, extra):
        s, part = [(3, 0), (1, 0), (2, 0), (3, 1), (2, 1), (1, 1)][k]
        out = half_of(self.stage(half, s), part)
        add_all(out, [half_of(self.own(half, s), part), half_of(self.near(half, s), part)] + extra)
        self.send(("row", half, k))

    def add_halves(self, s, *ks):
        self.await_pair(s)
        for half in range(self.halves):
            for k in ks:
                self.add_half(half, k, [])

    def add_final(self, out, half, extra, base):
        for part in range(2):
            terms = [half_of(self.own(half, 0), part), half_of(self.near(half, 0), part)]
            terms += [self.arrived(half, 1 + 3 * part), self.arrived(half, 2 + 3 * part)]
            terms += [half_of(ref, part) for ref in extra]
            add_all(half_of(out, part), terms, None if base is None else half_of(base, part))

    def run(self, place, panel, dst):
        halves, at = range(self.halves), self.at
        order = (3, 1, 2, 0)

        def give(s):
            for half in halves:
                self.send(("pair", half, s))

        def step(index):
            core = jnp.where(lax.rem(index, 2) == 0, 1 - at.core, at.core)
            row = choose(index // 2, [at.ring[s] for s in order])
            place([((half * 2 + core) * 4 + row) * self.block for half in halves], self.block)

        def then(*events):
            def event():
                for one in events:
                    one()

            return event

        after = {
            0: lambda: give(3),
            2: lambda: give(1),
            3: lambda: self.add_halves(3, 0, 3),
            4: then(lambda: give(2), lambda: self.add_halves(1, 1)),
            6: then(lambda: give(0), lambda: self.add_halves(2, 4)),
        }
        stepped(8, {}, step, after)
        for half in halves:
            self.land(("row", half, 0))
            self.add_half(half, 2, [self.arrived(half, 0)])
            self.land(("row", half, 3))
            self.add_half(half, 5, [self.arrived(half, 3)])
        self.await_pair(0)
        for half in halves:
            for k in (1, 4, 2, 5):
                self.land(("row", half, k))
        self.add_final(dst, 0, [], panel)
        self.finish()


STEPS = [(3, 0), (1, 0), (2, 0), (3, 1), (2, 1), (1, 1)]


class ReduceTwo(Sender):
    def __init__(self, at, term, near, stage, row_buf, z_buf, sems):
        super().__init__()
        self.at, self.term, self.sems = at, term, sems
        self.block = term.shape[0] // 16
        self.early = self.block * 3 // 8
        self.late = self.block - self.early
        self.near_buf, self.stage_buf, self.row_buf, self.z_buf = near, stage, row_buf, z_buf

    def start_of(self, half, core, s):
        return ((half * 2 + core) * 4 + self.at.ring[s]) * self.block

    def own(self, half, s):
        return rows_at(self.term, self.start_of(half, self.at.core, s), self.block)

    def near(self, half, s):
        return rows_at(self.near_buf, (half * 4 + s) * self.block, self.block)

    def window(self, kind, part=None):
        start, rows = (0, self.early) if kind == "early" else (self.early, self.late)
        return (start, rows) if part is None else (start + part * (rows // 2), rows // 2)

    def stage(self, kind, half, s, part=None):
        start, rows = self.window(kind, part)
        return rows_at(self.stage_buf, (half * 4 + s) * self.block + start, rows)

    def arrived(self, kind, half, k):
        rows = self.window(kind, 0)[1]
        if kind == "early":
            return rows_at(self.row_buf, self.late * 6 + k * rows, rows)
        return rows_at(self.row_buf, (half * 6 + k) * rows, rows)

    def crossed(self, s, part=None):
        start, rows = self.window("early", part)
        return rows_at(self.z_buf, s * self.early + start, rows)

    def last(self, index, part=None):
        rows = self.late if part is None else self.late // 2
        return rows_at(self.z_buf, 4 * self.early + index * self.late + (part or 0) * rows, rows)

    def copy(self, kind, half, k, arriving=False):
        pair_send, pair_recv, row_send, row_recv, z_send, z_recv = self.sems
        at = self.at
        if kind == "pair":
            away = rows_at(self.term, self.start_of(half, 1 - at.core, k), self.block)
            near = self.near(half, k)
            return push(near if arriving else away, near, pair_send.at[half, k], pair_recv.at[half, k], at.partner)
        if kind == "cross":
            src = self.crossed(k) if arriving else self.stage("early", 1 - at.upper, k)
            return push(src, self.crossed(k), z_send.at[k], z_recv.at[k], at.across)
        if kind == "last":
            return push(self.last(1 if arriving else 0), self.last(1), z_send.at[4], z_recv.at[4], at.across)
        peer = at.side if k in (0, 1, 5) else at.over
        s, part = STEPS[k]
        dst = self.arrived(kind, half, k)
        src = dst if arriving else self.stage(kind, at.upper if kind == "early" else half, s, part)
        group = 2 if kind == "early" else half
        return push(src, dst, row_send.at[group, k], row_recv.at[group, k], peer)

    def total(self, s):
        for half in range(2):
            self.land(("pair", half, s))
            out = rows_at(self.stage_buf, (half * 4 + s) * self.block, self.block)
            add_all(out, [self.own(half, s), self.near(half, s)])
        self.send(("cross", 0, s))

    def late_out(self, *ks):
        for half in range(2):
            for k in ks:
                self.send(("late", half, k))

    def late_next(self, before, k):
        s, part = STEPS[k]
        for half in range(2):
            self.land(("late", half, before))
            out = self.stage("late", half, s, part)
            add_all(out, [out, self.arrived("late", half, before)])
            self.send(("late", half, k))

    def early_out(self, k, before=None):
        s, part = STEPS[k]
        out = self.stage("early", self.at.upper, s, part)
        terms = [out, self.crossed(s, part)]
        if before is not None:
            self.land(("early", 0, before))
            terms.append(self.arrived("early", 0, before))
        add_all(out, terms)
        self.send(("early", 0, k))

    def ending(self, kind, out, half, extra, panel):
        for part in range(2):
            terms = [self.stage(kind, half, 0, part)]
            terms += [self.arrived(kind, half, 1 + 3 * part), self.arrived(kind, half, 2 + 3 * part)]
            terms.append(extra(part)) if extra else None
            start, rows = self.window(kind, part)
            if panel is None:
                add_all(self.last(0, part), terms)
            else:
                add_all(out.at[pl.ds(start, rows)], terms, panel.at[pl.ds(start, rows)])

    def run(self, place, panel, dst):
        at = self.at
        order = (3, 1, 2, 0)

        def give(s):
            for half in range(2):
                self.send(("pair", half, s))

        def step(index):
            core = jnp.where(lax.rem(index, 2) == 0, 1 - at.core, at.core)
            row = choose(index // 2, [at.ring[s] for s in order])
            place([((half * 2 + core) * 4 + row) * self.block for half in range(2)], self.block)

        def third():
            self.total(3)
            self.late_out(0, 3)

        def fourth():
            give(2)
            self.total(1)
            self.late_out(1)

        def sixth():
            give(0)
            self.total(2)
            self.late_out(4)

        after = {0: lambda: give(3), 2: lambda: give(1), 3: third, 4: fourth, 6: sixth}
        stepped(8, {}, step, after)
        self.land(("cross", 0, 3))
        self.early_out(0)
        self.early_out(3)
        self.late_next(0, 2)
        self.late_next(3, 5)
        self.total(0)
        self.land(("cross", 0, 1))
        self.early_out(1)
        self.land(("cross", 0, 2))
        self.early_out(4)
        self.early_out(2, 0)
        self.early_out(5, 3)
        for half in range(2):
            for k in (1, 4, 2, 5):
                self.land(("late", half, k))
        self.ending("late", None, 1 - at.upper, None, None)
        self.send(("last", 0, 0))
        self.land(("cross", 0, 0))
        for k in (1, 4, 2, 5):
            self.land(("early", 0, k))
        self.ending("early", dst, at.upper, lambda part: self.crossed(0, part), panel)
        self.land(("last", 0, 0))
        self.ending("late", dst, at.upper, lambda part: self.last(1, part), panel)
        self.finish()


def panel_kernel(
    low_hbm, mid_hbm, top_hbm, inv_low_hbm, inv_mid_hbm, inv_top_hbm, cpl_low_hbm, cpl_mid_hbm,
    parents_low, parents_mid,
    out_low, out_mid, out_top,
    inv_low, inv_mid, inv_top, cpl_low, cpl_mid, panel_mid, panel_top,
    buf_a, buf_b, buf_c, buf_t, near, stage, row_buf, z_buf, part, picked, wide,
    load, *sems,
):
    at = Place(4, 2)
    pulls = {}
    order = [
        ("low", low_hbm, rows_at(buf_a, at.row * low_hbm.shape[0], low_hbm.shape[0])),
        ("inv_low", inv_low_hbm, inv_low),
        ("cpl_low", cpl_low_hbm, cpl_low),
        ("panel_mid", mid_hbm, panel_mid),
        ("inv_mid", inv_mid_hbm, inv_mid),
        ("cpl_mid", cpl_mid_hbm, cpl_mid),
        ("panel_top", top_hbm, panel_top),
        ("inv_top", inv_top_hbm, inv_top),
    ]
    for index, (name, src, dst) in enumerate(order):
        pulls[name] = pltpu.make_async_copy(src, dst, load.at[index])

    def need(*names):
        for name in names:
            pulls.pop(name).wait()

    pulls["inv_low"].start()
    pulls["low"].start()
    at.greet()
    low_sems, mid_sems, mid_sems2, top_sems, top_sems2, low_red, top_red = (
        sems[0:6], sems[6:12], sems[12:18], sems[18:24], sems[24:30], sems[30:36], sems[36:42]
    )
    low = Exchange(at, buf_a, 0, low_sems, low_hbm)
    for piece in low.pieces():
        low.begin(*piece)
    low_targets = parents_low[pl.ds(at.group, 1), :]
    mid_targets = parents_mid[pl.ds(at.group // 2, 1), :]
    spread_lanes(wide, mid_targets)
    for total in (out_low, out_mid, out_top, picked):
        total[...] = jnp.zeros_like(total)
    need("low", "inv_low")
    for copy in pulls.values():
        copy.start()

    def user(matrix, panel, total, sign):
        def use(starts, depth):
            for start in starts:
                multiply(matrix, panel, total, start, depth, sign)

        return use

    def picker(panel):
        return lambda starts, depth: pick_add(picked, wide, panel, starts, depth)

    def placer(targets):
        return lambda starts, count: place_rows(buf_t, part, targets, starts, count)

    def begin(exchange, rows):
        for half, index in exchange.pieces():
            start, count = (half * exchange.sub + index) * exchange.count, exchange.count
            rows_at(exchange.buf, exchange.mine + start, count)[...] = rows(start, count).astype(jnp.bfloat16)
            exchange.begin(half, index)

    low.run(user(inv_low, buf_a, out_low, 1))

    need("cpl_low")
    couple_rows(cpl_low, out_low[...].astype(jnp.bfloat16), part)
    mid = Exchange(at, buf_b, 1, mid_sems)
    reduce_mid = Reduce(at, 1, buf_t, near, stage, row_buf, z_buf, low_red)
    need("panel_mid")
    reduce_mid.run(placer(low_targets), panel_mid, rows_at(buf_b, mid.mine, mid.block))
    mid.begin(0)
    mid.begin(1)
    need("inv_mid")
    mid.run(user(inv_mid, buf_b, out_mid, 1))

    need("cpl_mid")
    couple_rows(cpl_mid, out_mid[...].astype(jnp.bfloat16), part)
    top = Exchange(at, buf_c, 2, top_sems)
    reduce_top = ReduceTwo(at, buf_t, near, stage, row_buf, z_buf, top_red)
    need("panel_top")
    reduce_top.run(placer(mid_targets), panel_top, rows_at(buf_c, top.mine, top.block))
    top.begin(0)
    top.begin(1)
    need("inv_top")
    top.run(user(inv_top, buf_c, out_top, 1))

    back = Exchange(at, buf_t, 2, top_sems2)
    begin(back, lambda start, count: out_top[pl.ds(start, count), :])
    back.run(picker(buf_t))

    part[...] = picked[...].astype(jnp.bfloat16)
    lift = Exchange(at, buf_b, 1, mid_sems)
    begin(lift, lambda start, count: lift_rows(cpl_mid, part[...], start, count))
    spread_lanes(wide, low_targets)
    picked[...] = jnp.zeros_like(picked)
    lift.run(user(inv_mid, buf_b, out_mid, -1))

    back = Exchange(at, buf_c, 1, mid_sems2)
    begin(back, lambda start, count: out_mid[pl.ds(start, count), :])
    back.run(picker(buf_c))

    part[...] = picked[...].astype(jnp.bfloat16)
    lift = Exchange(at, buf_a, 0, low_sems)
    begin(lift, lambda start, count: lift_rows(cpl_low, part[...], start, count))
    lift.run(user(inv_low, buf_a, out_low, -1))


def settle_kernel(*refs):
    count = (len(refs) - 2) // 3
    sources, targets, held = refs[:count], refs[count : 2 * count], refs[2 * count : 3 * count]
    inward, outward = refs[3 * count :]
    pulls = [pltpu.make_async_copy(sources[i], held[i], inward.at[i]) for i in range(count)]
    pushes = [pltpu.make_async_copy(held[i], targets[i], outward.at[i]) for i in range(count)]
    for pull in pulls:
        pull.start()
    for pull, out in zip(pulls, pushes):
        pull.wait()
        out.start()
    for out in pushes:
        out.wait()


def settle(*arrays):
    count = len(arrays)
    return pl.pallas_call(
        settle_kernel,
        out_shape=tuple(jax.ShapeDtypeStruct(a.shape, a.dtype) for a in arrays),
        in_specs=[HBM_SPEC] * count,
        out_specs=(HBM_SPEC,) * count,
        scratch_shapes=[pltpu.VMEM(a.shape, a.dtype) for a in arrays] + [dma(count), dma(count)],
    )(*arrays)


def gather_sems(levels):
    units = 2 if levels >= 2 else 1
    return [dma(units, 12 if levels == 0 else 6)] * 2 + [dma(units, 8)] * 2 + [dma(2), dma(2)]


def reduce_sems(levels):
    pairs = [dma(levels, 4)] * 2
    return pairs + ([dma(3, 6)] * 2 + [dma(5)] * 2 if levels == 2 else [dma(1, 6)] * 2 + [dma(1)] * 2)


def solve_panel(
    panel_low, panel_mid, panel_top, inverse_low, inverse_mid, inverse_top, couple_low, couple_mid,
    parents_low, parents_mid,
):
    width = panel_low.shape[1]
    front, links = inverse_low.shape[2], couple_low.shape[1]

    def vmem(*shape, kind=jnp.bfloat16):
        return pltpu.VMEM(shape, kind)

    scratch = [vmem(*m.shape) for m in (inverse_low, inverse_mid, inverse_top, couple_low, couple_mid)]
    scratch += [vmem(*panel_mid.shape), vmem(*panel_top.shape)]
    scratch += [vmem(front, width)] * 4
    scratch += [vmem(front // 2, width)] * 2 + [vmem(front * 3 // 8, width), vmem(3 * panel_top.shape[0], width)]
    scratch += [vmem(links, width), vmem(links, width, kind=jnp.float32)]
    scratch += [vmem(links, 128, kind=jnp.int32), dma(8)]
    scratch += gather_sems(0) + gather_sems(1) * 2 + gather_sems(2) * 2
    scratch += reduce_sems(1) + reduce_sems(2)
    solved = pl.pallas_call(
        panel_kernel,
        out_shape=tuple(
            jax.ShapeDtypeStruct(p.shape, jnp.float32) for p in (panel_low, panel_mid, panel_top)
        ),
        in_specs=[HBM_SPEC] * 8 + [VMEM_SPEC] * 2,
        out_specs=(VMEM_SPEC,) * 3,
        scratch_shapes=scratch,
        compiler_params=params(7, 63),
    )(
        panel_low, panel_mid, panel_top, inverse_low, inverse_mid, inverse_top, couple_low, couple_mid,
        parents_low, parents_mid,
    )
    return settle(*solved)


def on_device(
    n,
    panel_low,
    panel_mid,
    panel_top,
    inverse_low,
    inverse_mid,
    inverse_top,
    couple_low,
    couple_mid,
    parents_low,
    parents_mid,
):
    if n == 4:
        return solve_panel(
            panel_low, panel_mid, panel_top, inverse_low, inverse_mid, inverse_top, couple_low, couple_mid,
            parents_low, parents_mid,
        )
    group = lax.axis_index("grp")
    low_targets = lax.dynamic_index_in_dim(parents_low, group, 0, keepdims=False)
    mid_targets = lax.dynamic_index_in_dim(parents_mid, group // 2, 0, keepdims=False)
    low_y = gather_solve(panel_low, inverse_low, n, 0, 0)
    term = spread_rows(complex_product(couple_low, low_y.astype(jnp.bfloat16)), low_targets)
    mid_y = reduce_solve(term, panel_mid, inverse_mid, n, 1, 1)
    term = spread_rows(complex_product(couple_mid, mid_y.astype(jnp.bfloat16)), mid_targets)
    top_x = reduce_solve(term, panel_top, inverse_top, n, 2, 2)
    top_full = gather(top_x.astype(jnp.bfloat16), n, 2, 3)
    lift = transposed_product(couple_mid, pick_rows(top_full, mid_targets)).astype(jnp.bfloat16)
    mid_x = mid_y - gather_solve(lift, inverse_mid, n, 1, 4)
    mid_full = gather(mid_x.astype(jnp.bfloat16), n, 1, 5)
    lift = transposed_product(couple_low, pick_rows(mid_full, low_targets)).astype(jnp.bfloat16)
    low_x = low_y - gather_solve(lift, inverse_low, n, 0, 6)
    return (low_x, mid_x, top_x)


def solution(mesh):
    placed = (
        P(("grp", "row"), None),
        P(("grp", "row"), None),
        P(("grp", "row"), None),
        P(None, ("grp", "row"), None),
        P(None, ("grp", "row"), None),
        P(None, ("grp", "row"), None),
        P(None, None, ("grp", "row")),
        P(None, None, ("grp", "row")),
        P(),
        P(),
    )
    return jax.shard_map(
        functools.partial(on_device, mesh.shape["row"]),
        mesh=mesh,
        in_specs=placed,
        out_specs=(P(("grp", "row"), None), P(("grp", "row"), None), P(("grp", "row"), None)),
        check_vma=False,
    )
```

```python
import functools
import math

import jax
import jax.numpy as jnp
from jax import lax
from jax.experimental import pallas as pl
from jax.experimental.pallas import tpu as pltpu
from jax.sharding import PartitionSpec as P

F = 4096
MESH = pl.DeviceIdType.MESH


def complex_product(matrix, panel):
    width = panel.shape[1] // 2
    real_term = jnp.dot(matrix[0], panel, preferred_element_type=jnp.float32)
    imag_term = jnp.dot(matrix[1], panel, preferred_element_type=jnp.float32)
    return real_term + jnp.concatenate([-imag_term[:, width:], imag_term[:, :width]], axis=1)


def transposed_product(matrix, panel):
    width = panel.shape[1] // 2
    contract = (((0,), (0,)), ((), ()))
    real_term = lax.dot_general(matrix[0], panel, contract, preferred_element_type=jnp.float32)
    imag_term = lax.dot_general(matrix[1], panel, contract, preferred_element_type=jnp.float32)
    return real_term + jnp.concatenate([-imag_term[:, width:], imag_term[:, :width]], axis=1)


class Place:
    def __init__(self, n, levels):
        self.n = n
        self.levels = levels
        self.square = n == 4
        self.group = lax.axis_index("grp")
        self.row = lax.axis_index("row")
        self.core = lax.rem(self.group, 2)
        self.upper = lax.rem(self.group // 2, 2)
        self.partner = (self.group + 1 - 2 * self.core, self.row)
        self.across = (self.group + 2 - 4 * self.upper, self.row)
        self.unit = lax.rem(self.group, 2**levels)
        if self.square:
            side = self.row + 1 - 2 * lax.rem(self.row, 2)
            over = self.row + 2 - 4 * (self.row // 2)
            self.ring = [self.row, side, over, 3 - self.row]
            self.side = (self.group, side)
            self.over = (self.group, over)

    def ahead(self, step):
        return self.ring[step] if self.square else lax.rem(self.row + step, self.n)

    def behind(self, step):
        return self.ring[step] if self.square else lax.rem(self.row + self.n - step, self.n)

    def greet(self):
        barrier = pltpu.get_barrier_semaphore()
        if self.square:
            peers = [self.side, self.over]
        else:
            peers = [(self.group, self.ahead(s)) for s in range(1, self.n)]
        if self.levels >= 1:
            peers.append(self.partner)
        if self.levels >= 2:
            peers.append(self.across)
        for peer in peers:
            pl.semaphore_signal(barrier, inc=1, device_id=peer, device_id_type=MESH)
        pl.semaphore_wait(barrier, len(peers))


def push(src, dst, send, recv, peer):
    return pltpu.make_async_remote_copy(
        src_ref=src, dst_ref=dst, send_sem=send, recv_sem=recv, device_id=peer, device_id_type=MESH
    )


def half_of(ref, index):
    rows = ref.shape[0] // 2
    return ref.at[pl.ds(index * rows, rows)]


def spread(at, out, sems, use):
    n, levels = at.n, at.levels
    row_send, row_recv, pair_send, pair_recv, z_send, z_recv = sems
    near = at.unit
    started = []

    def go(src, send, recv, peer):
        copy = push(src, src, send, recv, peer)
        copy.start()
        started.append(copy)

    def landed(ref, send, recv, peer):
        push(ref, ref, send, recv, peer).wait_recv()

    def row_copy(act, which, k, slot, half, peer):
        act(half_of(out.at[slot], half), row_send.at[which, k], row_recv.at[which, k], peer)

    def to_rows(which, unit):
        mine = unit * n + at.row
        if at.square:
            row_copy(go, which, 0, mine, 0, at.side)
            row_copy(go, which, 1, mine, 1, at.over)
            row_copy(go, which, 2, mine, 1, at.side)
            row_copy(go, which, 3, mine, 0, at.over)
            return
        for s in range(1, n):
            go(out.at[mine], row_send.at[which, s], row_recv.at[which, s], (at.group, at.ahead(s)))

    def forward(which, unit):
        if at.square:
            side, over = unit * n + at.ring[1], unit * n + at.ring[2]
            row_copy(landed, which, 0, side, 0, at.side)
            row_copy(go, which, 4, side, 0, at.over)
            row_copy(landed, which, 1, over, 1, at.over)
            row_copy(go, which, 5, over, 1, at.side)

    def await_row(which, unit, s):
        slot = unit * n + at.behind(s)
        if not at.square:
            peer = (at.group, at.behind(s))
            landed(out.at[slot], row_send.at[which, s], row_recv.at[which, s], peer)
        elif s == 1:
            row_copy(landed, which, 2, slot, 1, at.side)
        elif s == 2:
            row_copy(landed, which, 3, slot, 0, at.over)
        else:
            row_copy(landed, which, 4, slot, 0, at.over)
            row_copy(landed, which, 5, slot, 1, at.side)

    def to_pair(which, s, unit):
        src = out.at[unit * n + at.behind(s)]
        go(src, pair_send.at[which, s], pair_recv.at[which, s], at.partner)

    def await_pair(which, s, unit):
        slot = (unit + 1 - 2 * at.core) * n + at.behind(s)
        landed(out.at[slot], pair_send.at[which, s], pair_recv.at[which, s], at.partner)
        use(slot)

    units = [near]
    if levels >= 2:
        units.append(lax.rem(near + 2, 4))
        go(out.at[near * n + at.row], z_send.at[0], z_recv.at[0], at.across)
    to_rows(0, near)
    if levels >= 1:
        to_pair(0, 0, near)
    if levels >= 2:
        landed(out.at[units[1] * n + at.row], z_send.at[0], z_recv.at[0], at.across)
        to_rows(1, units[1])
        to_pair(1, 0, units[1])
    use(near * n + at.row)
    if levels >= 2:
        use(units[1] * n + at.row)
    for which, unit in enumerate(units):
        forward(which, unit)
    for s in range(1, n):
        for which, unit in enumerate(units):
            await_row(which, unit, s)
            if levels >= 1:
                to_pair(which, s, unit)
                await_pair(which, s - 1, unit)
            use(unit * n + at.behind(s))
    if levels >= 1:
        for which, unit in enumerate(units):
            await_pair(which, n - 1, unit)
    for copy in started:
        copy.wait_send()


def solver(n, out, inverse_hbm, inverse, turned, total, sem):
    count, block, width = out.shape
    rows = inverse.shape[1]
    tile = min(rows, 256)
    whole = block % 128 == 0
    together = 1 if whole else turned.shape[0] // block
    copy = pltpu.make_async_copy(inverse_hbm, inverse, sem)
    copy.start()
    waiting = [copy]

    def multiply(slot, first):
        panel = out[slot] if whole else out[pl.ds(slot, together)].reshape(turned.shape)
        half = width // 2
        turned[:, :half] = -panel[:, half:]
        turned[:, half:] = panel[:, :half]
        span_columns = turned.shape[0]
        columns = pl.ds(pl.multiple_of(slot // together * span_columns, span_columns), span_columns)

        def body(index, carry):
            span = pl.ds(pl.multiple_of(index * tile, tile), tile)
            block_now = out[slot] if whole else panel
            real = jnp.dot(inverse[0, span, columns], block_now, preferred_element_type=jnp.float32)
            imag = jnp.dot(inverse[1, span, columns], turned[...], preferred_element_type=jnp.float32)
            if first:
                total[span, :] = real + imag
            else:
                total[span, :] = total[span, :] + (real + imag)
            return carry

        lax.fori_loop(0, rows // tile, body, 0)

    def use(slot):
        if whole:
            first = bool(waiting)
            if first:
                waiting.pop().wait()
            multiply(slot, first)

    def rest():
        if not whole:
            waiting.pop().wait()
            for slot in range(0, count, together):
                multiply(slot, slot == 0)

    return use, rest


def gather_kernel(n, levels, own, full, *sems):
    at = Place(n, levels)
    at.greet()
    full[at.unit * n + at.row] = own[...]
    spread(at, full, sems, lambda slot: None)


def gather_solve_kernel(n, levels, own, inverse_hbm, total, full, inverse, turned, sem, *sems):
    at = Place(n, levels)
    use, rest = solver(n, full, inverse_hbm, inverse, turned, total, sem)
    at.greet()
    full[at.unit * n + at.row] = own[...]
    spread(at, full, sems, use)
    rest()


def add_rows(out_ref, terms, panel=None):
    rows = out_ref.shape[0]
    step = min(rows, 64)

    def body(index, carry):
        span = pl.ds(pl.multiple_of(index * step, step), step)
        total = terms[0][span, :].astype(jnp.float32)
        for term in terms[1:]:
            total = total + term[span, :].astype(jnp.float32)
        if panel is not None:
            total = panel[span, :].astype(jnp.float32) - total
        out_ref[span, :] = total.astype(out_ref.dtype)
        return carry

    lax.fori_loop(0, rows // step, body, 0)


def reduce_solve_kernel(
    n, levels, term, panel, inverse_hbm, total, full, inverse, turned, near_buf, stage, row_buf, z_buf, sem, *sems
):
    at = Place(n, levels)
    halves = 2 ** (levels - 1)
    spread_sems = sems[:6]
    pair_send, pair_recv, row_send, row_recv, z_send, z_recv = sems[6:]
    use, finish_solve = solver(n, full, inverse_hbm, inverse, turned, total, sem)
    at.greet()
    started = []

    def go(src, dst, send, recv, peer):
        copy = push(src, dst, send, recv, peer)
        copy.start()
        started.append(copy)

    def landed(ref, send, recv, peer):
        push(ref, ref, send, recv, peer).wait_recv()

    order = [3, 1, 2, 0] if at.square else list(range(1, n)) + [0]
    for s in order:
        for half in range(halves):
            src = term.at[(half * 2 + 1 - at.core) * n + at.ahead(s)]
            go(src, near_buf.at[half, s], pair_send.at[half, s], pair_recv.at[half, s], at.partner)

    def own_term(half, s):
        return term.at[(half * 2 + at.core) * n + at.ahead(s)]

    def await_pair(half, s):
        landed(near_buf.at[half, s], pair_send.at[half, s], pair_recv.at[half, s], at.partner)

    def row_copy(half, k, src, peer):
        go(src, row_buf.at[half, k], row_send.at[half, k], row_recv.at[half, k], peer)

    def await_row(half, k, peer):
        landed(row_buf.at[half, k], row_send.at[half, k], row_recv.at[half, k], peer)

    if at.square:
        for half in range(halves):
            await_pair(half, 3)
            add_rows(stage.at[half, 3], [own_term(half, 3), near_buf.at[half, 3]])
            row_copy(half, 0, half_of(stage.at[half, 3], 0), at.side)
            row_copy(half, 3, half_of(stage.at[half, 3], 1), at.over)
        for half in range(halves):
            await_pair(half, 1)
            first = half_of(stage.at[half, 1], 0)
            add_rows(first, [half_of(own_term(half, 1), 0), half_of(near_buf.at[half, 1], 0)])
            row_copy(half, 1, first, at.side)
            await_pair(half, 2)
            second = half_of(stage.at[half, 2], 1)
            add_rows(second, [half_of(own_term(half, 2), 1), half_of(near_buf.at[half, 2], 1)])
            row_copy(half, 4, second, at.over)
        for half in range(halves):
            await_row(half, 0, at.side)
            first = half_of(stage.at[half, 2], 0)
            near = half_of(near_buf.at[half, 2], 0)
            add_rows(first, [half_of(own_term(half, 2), 0), near, row_buf.at[half, 0]])
            row_copy(half, 2, first, at.over)
            await_row(half, 3, at.over)
            second = half_of(stage.at[half, 1], 1)
            near = half_of(near_buf.at[half, 1], 1)
            add_rows(second, [half_of(own_term(half, 1), 1), near, row_buf.at[half, 3]])
            row_copy(half, 5, second, at.side)
        for half in range(halves):
            await_pair(half, 0)
            await_row(half, 1, at.side)
            await_row(half, 4, at.over)
            await_row(half, 2, at.over)
            await_row(half, 5, at.side)
    else:
        for s in range(1, n):
            for half in range(halves):
                await_pair(half, s)
                add_rows(stage.at[half, s], [own_term(half, s), near_buf.at[half, s]])
                row_copy(half, s, stage.at[half, s], (at.group, at.ahead(s)))
        for half in range(halves):
            await_pair(half, 0)
            for s in range(1, n):
                await_row(half, s, (at.group, at.behind(s)))

    def finish(dst, half, extra, base):
        own, near = own_term(half, 0), near_buf.at[half, 0]
        if not at.square:
            rest = [row_buf.at[half, s] for s in range(1, n)]
            add_rows(dst, [own, near] + rest + extra, base)
            return
        for part in range(2):
            rest = [row_buf.at[half, 1 + 3 * part], row_buf.at[half, 2 + 3 * part]]
            rest = rest + [half_of(ref, part) for ref in extra]
            terms = [half_of(own, part), half_of(near, part)] + rest
            add_rows(half_of(dst, part), terms, None if base is None else half_of(base, part))

    slot = at.unit * n + at.row
    if levels == 1:
        finish(full.at[slot], 0, [], panel)
    else:
        finish(z_buf.at[0], 1 - at.upper, [], None)
        go(z_buf.at[0], z_buf.at[1], z_send.at[0], z_recv.at[0], at.across)
        landed(z_buf.at[1], z_send.at[0], z_recv.at[0], at.across)
        finish(full.at[slot], at.upper, [z_buf.at[1]], panel)
    spread(at, full, spread_sems, use)
    finish_solve()
    for copy in started:
        copy.wait_send()


def dma(*shape):
    return pltpu.SemaphoreType.DMA(shape)


VMEM_SPEC = pl.BlockSpec(memory_space=pltpu.VMEM)
HBM_SPEC = pl.BlockSpec(memory_space=pltpu.HBM)


def spread_scratch(n):
    k = max(n, 6)
    return [dma(2, k), dma(2, k), dma(2, n), dma(2, n), dma(1), dma(1)]


def params(ident, mebibytes):
    return pltpu.CompilerParams(
        collective_id=ident, has_side_effects=True, vmem_limit_bytes=mebibytes << 20
    )


def gather(own, n, levels, ident):
    block, width = own.shape
    count = 2**levels * n
    full = pl.pallas_call(
        functools.partial(gather_kernel, n, levels),
        out_shape=jax.ShapeDtypeStruct((count, block, width), own.dtype),
        in_specs=[VMEM_SPEC],
        out_specs=VMEM_SPEC,
        scratch_shapes=spread_scratch(n),
        compiler_params=params(ident, 16),
    )(own)
    return full.reshape(count * block, width)


def solve_scratch(inverse, block, width, count):
    return [
        pltpu.VMEM((count, block, width), jnp.bfloat16),
        pltpu.VMEM(inverse.shape, inverse.dtype),
        pltpu.VMEM((block if block % 128 == 0 else 512, width), jnp.bfloat16),
    ]


def gather_solve(own, inverse, n, levels, ident):
    block, width = own.shape
    return pl.pallas_call(
        functools.partial(gather_solve_kernel, n, levels),
        out_shape=jax.ShapeDtypeStruct((inverse.shape[1], width), jnp.float32),
        in_specs=[VMEM_SPEC, HBM_SPEC],
        out_specs=VMEM_SPEC,
        scratch_shapes=solve_scratch(inverse, block, width, 2**levels * n)
        + [pltpu.SemaphoreType.DMA]
        + spread_scratch(n),
        compiler_params=params(ident, 32),
    )(own, inverse)


def reduce_solve(term, panel, inverse, n, levels, ident):
    block, width = panel.shape
    count = 2**levels * n
    halves = 2 ** (levels - 1)
    whole = pltpu.VMEM((halves, n, block, width), jnp.bfloat16)
    if n == 4:
        pieces, k = pltpu.VMEM((halves, 6, block // 2, width), jnp.bfloat16), 6
    else:
        pieces, k = whole, n
    return pl.pallas_call(
        functools.partial(reduce_solve_kernel, n, levels),
        out_shape=jax.ShapeDtypeStruct((inverse.shape[1], width), jnp.float32),
        in_specs=[VMEM_SPEC, VMEM_SPEC, HBM_SPEC],
        out_specs=VMEM_SPEC,
        scratch_shapes=solve_scratch(inverse, block, width, count)
        + [whole, whole, pieces, pltpu.VMEM((2, block, width), jnp.bfloat16)]
        + [pltpu.SemaphoreType.DMA]
        + spread_scratch(n)
        + [dma(halves, n), dma(halves, n), dma(halves, k), dma(halves, k), dma(1), dma(1)],
        compiler_params=params(ident, 32),
    )(term.reshape(count, block, width), panel, inverse)


def spread_kernel(tile, targets, rows, out):
    index = lax.broadcasted_iota(jnp.int32, (tile, 1), 0) + pl.program_id(0) * tile
    marks = (index == targets[...]).astype(jnp.float32).astype(jnp.bfloat16)
    out[...] = jnp.dot(marks, rows[...], preferred_element_type=jnp.float32).astype(out.dtype)


def spread_rows(partial_rows, targets):
    count, width = partial_rows.shape
    tile = F // 4
    return pl.pallas_call(
        functools.partial(spread_kernel, tile),
        grid=(F // tile,),
        in_specs=[
            pl.BlockSpec((1, count), lambda i: (0, 0)),
            pl.BlockSpec((count, width), lambda i: (0, 0)),
        ],
        out_specs=pl.BlockSpec((tile, width), lambda i: (i, 0)),
        out_shape=jax.ShapeDtypeStruct((F, width), jnp.bfloat16),
        compiler_params=pltpu.CompilerParams(vmem_limit_bytes=32 << 20),
    )(targets[None, :], partial_rows.astype(jnp.bfloat16))


def pick_rows(panel, targets):
    marks = (targets[:, None] == lax.broadcasted_iota(jnp.int32, (1, F), 1)).astype(jnp.bfloat16)
    return jnp.dot(marks, panel, preferred_element_type=jnp.float32).astype(jnp.bfloat16)


def dot32(left, right):
    return jnp.dot(left, right, preferred_element_type=jnp.float32)


def turn(product):
    half, width = product.shape[0] // 2, product.shape[1] // 2
    real, imag = product[:half], product[half:]
    return real + jnp.concatenate([-imag[:, width:], imag[:, :width]], axis=1)


def rows_at(ref, start, count):
    return ref.at[pl.ds(pl.multiple_of(start, math.gcd(count, 256)), count)]


def multiply(matrix, panel, total, start, depth, sign):
    rows = matrix.shape[1]
    tile = min(rows, 512)
    span = pl.ds(pl.multiple_of(start, depth), depth)
    block = panel[span, :]
    for base in range(0, rows, tile):
        part = pl.ds(base, tile)
        left = matrix[:, part, span].reshape(2 * tile, depth)
        product = turn(dot32(left, block))
        total[part, :] = total[part, :] + product if sign > 0 else total[part, :] - product


def choose(index, values):
    out = values[-1]
    for k in range(len(values) - 2, -1, -1):
        out = jnp.where(index == k, values[k], out)
    return out


def stepped(count, before, step, after):
    def body(index, carry):
        for k, event in before.items():
            pl.when(index == k)(event)
        step(index)
        for k, event in after.items():
            pl.when(index == k)(event)
        return carry

    lax.fori_loop(0, count, body, 0)


def couple_rows(matrix, panel, out):
    tile = 1024
    for base in range(0, matrix.shape[1], tile):
        part = pl.ds(base, tile)
        left = matrix[:, part, :].reshape(2 * tile, matrix.shape[2])
        out[part, :] = turn(dot32(left, panel)).astype(out.dtype)


def lift_rows(matrix, panel, start, count):
    columns = pl.ds(start, count)
    contract = (((0,), (0,)), ((), ()))
    real = lax.dot_general(matrix[0, :, columns], panel, contract, preferred_element_type=jnp.float32)
    imag = lax.dot_general(matrix[1, :, columns], panel, contract, preferred_element_type=jnp.float32)
    width = panel.shape[1] // 2
    return real + jnp.concatenate([-imag[:, width:], imag[:, :width]], axis=1)


def place_rows(term, part, targets, starts, count):
    iota = lax.broadcasted_iota(jnp.int32, (count, 1), 0)
    marks = [(iota + start == targets).astype(jnp.float32).astype(jnp.bfloat16) for start in starts]
    placed = dot32(jnp.concatenate(marks, axis=0), part[...])
    for index, start in enumerate(starts):
        rows_at(term, start, count)[...] = placed[index * count : (index + 1) * count].astype(term.dtype)


def spread_lanes(wide, targets):
    for base in range(0, wide.shape[0], 128):
        square = jnp.broadcast_to(targets[:, base : base + 128], (128, 128))
        wide[pl.ds(base, 128), :] = square.T


def pick_add(total, wide, panel, starts, depth):
    blocks = [panel[pl.ds(pl.multiple_of(start, depth), depth), :] for start in starts]
    block = jnp.concatenate(blocks, axis=0) if len(blocks) > 1 else blocks[0]
    lanes = lax.broadcasted_iota(jnp.int32, (1, 128), 1)
    tile = 1024
    for base in range(0, wide.shape[0], tile):
        part = pl.ds(base, tile)
        wanted = wide[part, :]
        marks = []
        for start in starts:
            for shift in range(0, depth, 128):
                marks.append((lanes + (start + shift) == wanted).astype(jnp.float32).astype(jnp.bfloat16))
        total[part, :] = total[part, :] + dot32(jnp.concatenate(marks, axis=1), block)


def add_all(out, terms, base=None):
    total = terms[0][...].astype(jnp.float32)
    for term in terms[1:]:
        total = total + term[...].astype(jnp.float32)
    if base is not None:
        total = base[...].astype(jnp.float32) - total
    out[...] = total.astype(out.dtype)


class Sender:
    def __init__(self):
        self.log = {}

    def send(self, key):
        self.copy(*key).start()
        self.log[key] = True

    def land(self, key):
        self.copy(*key, arriving=True).wait_recv()

    def sent(self, *keys):
        for key in keys:
            del self.log[key]
            self.copy(*key).wait_send()

    def finish(self):
        self.sent(*list(self.log))


class Exchange(Sender):
    def __init__(self, at, buf, levels, sems, source=None):
        super().__init__()
        self.at, self.buf, self.levels, self.sems, self.source = at, buf, levels, sems, source
        self.block = buf.shape[0] // (4 * 2**levels)
        self.sub = 2 if levels == 0 else 1
        self.count = self.block // (2 * self.sub)
        near = lax.rem(at.group, 2**levels)
        self.units = [near]
        if levels >= 2:
            self.units.append(lax.rem(near + 2, 4))
        self.mine = self.start_of(near, 0)

    def start_of(self, unit, s):
        return (unit * 4 + self.at.ring[s]) * self.block

    def copy(self, kind, which, a, b, arriving=False):
        row_send, row_recv, pair_send, pair_recv, z_send, z_recv = self.sems
        at, unit, index = self.at, self.units[which], 0
        if kind == "row":
            link, stage, index = a, b // self.sub, b % self.sub
            outward = [(0, link), (0, 1 - link), (2 - link, 1 - link)]
            inward = [(1 + link, link), (1 + link, 1 - link), (3, 1 - link)]
            s, half = (inward if arriving else outward)[stage]
            k, peer = link * 3 * self.sub + b, at.over if link else at.side
            send, recv = row_send.at[which, k], row_recv.at[which, k]
        elif kind == "pair":
            s, half = a, b
            send, recv, peer = pair_send.at[which, 2 * s + half], pair_recv.at[which, 2 * s + half], at.partner
            unit = unit + 1 - 2 * at.core if arriving else unit
        else:
            s, half = 0, b
            send, recv, peer = z_send.at[half], z_recv.at[half], at.across
            unit = self.units[1] if arriving else self.units[0]
        shift = (half * self.sub + index) * self.count
        ref = rows_at(self.buf, self.start_of(unit, s) + shift, self.count)
        src = ref
        if self.source is not None and s == 0 and not arriving:
            src = self.source.at[pl.ds(shift, self.count)]
        return push(src, ref, send, recv, peer)

    def pieces(self):
        return [(half, index) for index in range(self.sub) for half in range(2)]

    def begin(self, half, index=0):
        self.send(("row", 0, half, index))
        if self.levels == 0:
            self.send(("row", 0, 1 - half, self.sub + index))
        if self.levels >= 2:
            self.send(("z", 0, 0, half))
        if self.levels >= 1:
            self.send(("pair", 0, 0, half))

    def arrive(self, which, link, stage, index=0):
        self.land(("row", which, link, stage * self.sub + index))
        if stage == 0:
            self.send(("row", which, 1 - link, 2 * self.sub + index))
        if self.levels >= 1:
            s, half = [(1 + link, link), (1 + link, 1 - link), (3, 1 - link)][stage]
            self.send(("pair", which, s, half))

    def both(self, which, stage):
        for link, index in self.pieces():
            self.arrive(which, link, stage, index)

    def second(self, which):
        for link, index in self.pieces():
            self.sent(("row", which, link, index))
            self.send(("row", which, link, self.sub + index))

    def await_pair(self, which, *rows):
        for s in rows:
            for half in range(2):
                self.land(("pair", which, s, half))

    def z_first(self):
        for half in range(2):
            self.land(("z", 0, 0, half))
            self.send(("row", 1, half, 0))
            self.send(("pair", 1, 0, half))

    def run(self, use):
        def block(which, other, s):
            return self.start_of(self.units[which] + (1 - 2 * self.at.core) * other, s)

        def then(*events):
            def event():
                for call, *arguments in events:
                    call(*arguments)

            return event

        if self.levels == 0:
            order = [(0, 0), (0, 1), (0, 2), (0, 3), (1, 0), (2, 2), (1, 1), (2, 3)]
            order += [(1, 2), (2, 0), (1, 3), (2, 1), (3, 0), (3, 2), (3, 1), (3, 3)]
            starts = [[block(0, 0, s) + piece * self.count for s, piece in order]]
            depth = self.count
            before = {4: then((self.both, 0, 0)), 8: then((self.both, 0, 1))}
            for step, (link, index) in ((12, (1, 0)), (13, (0, 0)), (14, (1, 1)), (15, (0, 1))):
                before[step] = then((self.arrive, 0, link, 2, index))
        elif self.levels == 1:
            halves = [
                [(0, 0, 0), (1, 0, 0), (0, 1, 0), (1, 1, 0), (0, 1, 1), (1, 1, 1), (0, 3, 0), (1, 3, 0)],
                [(0, 0, 1), (1, 0, 1), (0, 2, 1), (1, 2, 1), (0, 2, 0), (1, 2, 0), (0, 3, 1), (1, 3, 1)],
            ]
            starts = [[block(0, other, s) + half * self.count for other, s, half in line] for line in halves]
            depth = self.count
            before = {
                1: then((self.await_pair, 0, 0)),
                2: then((self.second, 0), (self.both, 0, 0)),
                3: then((self.land, ("pair", 0, 1, 0)), (self.land, ("pair", 0, 2, 1))),
                4: then((self.both, 0, 1)),
                5: then((self.land, ("pair", 0, 1, 1)), (self.land, ("pair", 0, 2, 0))),
                6: then((self.both, 0, 2)),
                7: then((self.await_pair, 0, 3)),
            }
        else:
            starts = [
                [block(*b) for b in line]
                for line in (
                    [(0, 0, 0), (0, 0, 1), (0, 1, 1), (1, 0, 0), (0, 0, 3), (1, 0, 1), (1, 1, 1), (1, 0, 3)],
                    [(0, 1, 0), (0, 0, 2), (0, 1, 2), (1, 1, 0), (0, 1, 3), (1, 0, 2), (1, 1, 2), (1, 1, 3)],
                )
            ]
            depth = self.block
            before = {
                0: then((self.await_pair, 0, 0)),
                1: then((self.second, 0), (self.both, 0, 0), (self.z_first,), (self.both, 0, 1)),
                2: then((self.await_pair, 0, 1, 2)),
                3: then((self.second, 1), (self.both, 0, 2), (self.await_pair, 1, 0)),
                4: then((self.both, 1, 0), (self.await_pair, 0, 3)),
                5: then((self.both, 1, 1)),
                6: then((self.both, 1, 2), (self.await_pair, 1, 1, 2)),
                7: then((self.await_pair, 1, 3)),
            }
        count = len(starts[0])
        stepped(count, before, lambda i: use([choose(i, line) for line in starts], depth), {})
        self.finish()


class Reduce(Sender):
    def __init__(self, at, levels, term, near, stage, row_buf, z_buf, sems):
        super().__init__()
        self.at, self.levels, self.term, self.sems = at, levels, term, sems
        self.halves = 2 ** (levels - 1)
        self.block = term.shape[0] // (8 * self.halves)
        self.near_buf, self.stage_buf, self.row_buf, self.z_buf = near, stage, row_buf, z_buf

    def start_of(self, half, core, s):
        return ((half * 2 + core) * 4 + self.at.ring[s]) * self.block

    def own(self, half, s):
        return rows_at(self.term, self.start_of(half, self.at.core, s), self.block)

    def near(self, half, s):
        return rows_at(self.near_buf, (half * 4 + s) * self.block, self.block)

    def stage(self, half, s):
        return rows_at(self.stage_buf, (half * 4 + s) * self.block, self.block)

    def arrived(self, half, k):
        rows = self.block // 2
        return rows_at(self.row_buf, (half * 6 + k) * rows, rows)

    def copy(self, kind, half, k, arriving=False):
        pair_send, pair_recv, row_send, row_recv, z_send, z_recv = self.sems
        at = self.at
        if kind == "pair":
            away = rows_at(self.term, self.start_of(half, 1 - at.core, k), self.block)
            near = self.near(half, k)
            return push(near if arriving else away, near, pair_send.at[half, k], pair_recv.at[half, k], at.partner)
        if kind == "row":
            peer = at.side if k in (0, 1, 5) else at.over
            s, part = [(3, 0), (1, 0), (2, 0), (3, 1), (2, 1), (1, 1)][k]
            src = self.arrived(half, k) if arriving else half_of(self.stage(half, s), part)
            return push(src, self.arrived(half, k), row_send.at[half, k], row_recv.at[half, k], peer)
        mine, theirs = half_of(self.z_buf, 0), half_of(self.z_buf, 1)
        return push(theirs if arriving else mine, theirs, z_send.at[0], z_recv.at[0], at.across)

    def await_pair(self, s):
        for half in range(self.halves):
            self.land(("pair", half, s))

    def add_half(self, half, k, extra):
        s, part = [(3, 0), (1, 0), (2, 0), (3, 1), (2, 1), (1, 1)][k]
        out = half_of(self.stage(half, s), part)
        add_all(out, [half_of(self.own(half, s), part), half_of(self.near(half, s), part)] + extra)
        self.send(("row", half, k))

    def add_halves(self, s, *ks):
        self.await_pair(s)
        for half in range(self.halves):
            for k in ks:
                self.add_half(half, k, [])

    def add_final(self, out, half, extra, base):
        for part in range(2):
            terms = [half_of(self.own(half, 0), part), half_of(self.near(half, 0), part)]
            terms += [self.arrived(half, 1 + 3 * part), self.arrived(half, 2 + 3 * part)]
            terms += [half_of(ref, part) for ref in extra]
            add_all(half_of(out, part), terms, None if base is None else half_of(base, part))

    def run(self, place, panel, dst):
        halves, at = range(self.halves), self.at
        order = (3, 1, 2, 0)

        def give(s):
            for half in halves:
                self.send(("pair", half, s))

        def step(index):
            core = jnp.where(lax.rem(index, 2) == 0, 1 - at.core, at.core)
            row = choose(index // 2, [at.ring[s] for s in order])
            place([((half * 2 + core) * 4 + row) * self.block for half in halves], self.block)

        def then(*events):
            def event():
                for one in events:
                    one()

            return event

        after = {
            0: lambda: give(3),
            2: then(lambda: give(1), lambda: self.add_halves(3, 0, 3)),
            4: then(lambda: give(2), lambda: self.add_halves(1, 1)),
            6: then(lambda: give(0), lambda: self.add_halves(2, 4)),
        }
        stepped(8, {}, step, after)
        for half in halves:
            self.land(("row", half, 0))
            self.add_half(half, 2, [self.arrived(half, 0)])
            self.land(("row", half, 3))
            self.add_half(half, 5, [self.arrived(half, 3)])
        self.await_pair(0)
        for half in halves:
            for k in (1, 4, 2, 5):
                self.land(("row", half, k))
        self.add_final(dst, 0, [], panel)
        self.finish()


STEPS = [(3, 0), (1, 0), (2, 0), (3, 1), (2, 1), (1, 1)]


class ReduceTwo(Sender):
    def __init__(self, at, term, near, stage, row_buf, z_buf, sems):
        super().__init__()
        self.at, self.term, self.sems = at, term, sems
        self.block = term.shape[0] // 16
        self.early = self.block // 2
        self.late = self.block - self.early
        self.near_buf, self.stage_buf, self.row_buf, self.z_buf = near, stage, row_buf, z_buf

    def start_of(self, half, core, s):
        return ((half * 2 + core) * 4 + self.at.ring[s]) * self.block

    def own(self, half, s):
        return rows_at(self.term, self.start_of(half, self.at.core, s), self.block)

    def near(self, half, s):
        return rows_at(self.near_buf, (half * 4 + s) * self.block, self.block)

    def window(self, kind, part=None):
        start, rows = (0, self.early) if kind == "early" else (self.early, self.late)
        return (start, rows) if part is None else (start + part * (rows // 2), rows // 2)

    def stage(self, kind, half, s, part=None):
        start, rows = self.window(kind, part)
        return rows_at(self.stage_buf, (half * 4 + s) * self.block + start, rows)

    def arrived(self, kind, half, k):
        rows = self.window(kind, 0)[1]
        if kind == "early":
            return rows_at(self.row_buf, self.late * 6 + k * rows, rows)
        return rows_at(self.row_buf, (half * 6 + k) * rows, rows)

    def crossed(self, s, part=None):
        start, rows = self.window("early", part)
        return rows_at(self.z_buf, s * self.early + start, rows)

    def last(self, index, part=None):
        rows = self.late if part is None else self.late // 2
        return rows_at(self.z_buf, 4 * self.early + index * self.late + (part or 0) * rows, rows)

    def copy(self, kind, half, k, arriving=False):
        pair_send, pair_recv, row_send, row_recv, z_send, z_recv = self.sems
        at = self.at
        if kind == "pair":
            away = rows_at(self.term, self.start_of(half, 1 - at.core, k), self.block)
            near = self.near(half, k)
            return push(near if arriving else away, near, pair_send.at[half, k], pair_recv.at[half, k], at.partner)
        if kind == "cross":
            src = self.crossed(k) if arriving else self.stage("early", 1 - at.upper, k)
            return push(src, self.crossed(k), z_send.at[k], z_recv.at[k], at.across)
        if kind == "last":
            return push(self.last(1 if arriving else 0), self.last(1), z_send.at[4], z_recv.at[4], at.across)
        peer = at.side if k in (0, 1, 5) else at.over
        s, part = STEPS[k]
        dst = self.arrived(kind, half, k)
        src = dst if arriving else self.stage(kind, at.upper if kind == "early" else half, s, part)
        group = 2 if kind == "early" else half
        return push(src, dst, row_send.at[group, k], row_recv.at[group, k], peer)

    def total(self, s):
        for half in range(2):
            self.land(("pair", half, s))
            out = rows_at(self.stage_buf, (half * 4 + s) * self.block, self.block)
            add_all(out, [self.own(half, s), self.near(half, s)])
        self.send(("cross", 0, s))

    def late_out(self, *ks):
        for half in range(2):
            for k in ks:
                self.send(("late", half, k))

    def late_next(self, before, k):
        s, part = STEPS[k]
        for half in range(2):
            self.land(("late", half, before))
            out = self.stage("late", half, s, part)
            add_all(out, [out, self.arrived("late", half, before)])
            self.send(("late", half, k))

    def early_out(self, k, before=None):
        s, part = STEPS[k]
        out = self.stage("early", self.at.upper, s, part)
        terms = [out, self.crossed(s, part)]
        if before is not None:
            self.land(("early", 0, before))
            terms.append(self.arrived("early", 0, before))
        add_all(out, terms)
        self.send(("early", 0, k))

    def ending(self, kind, out, half, extra, panel):
        for part in range(2):
            terms = [self.stage(kind, half, 0, part)]
            terms += [self.arrived(kind, half, 1 + 3 * part), self.arrived(kind, half, 2 + 3 * part)]
            terms.append(extra(part)) if extra else None
            start, rows = self.window(kind, part)
            if panel is None:
                add_all(self.last(0, part), terms)
            else:
                add_all(out.at[pl.ds(start, rows)], terms, panel.at[pl.ds(start, rows)])

    def run(self, place, panel, dst):
        at = self.at
        order = (3, 1, 2, 0)

        def give(s):
            for half in range(2):
                self.send(("pair", half, s))

        def step(index):
            core = jnp.where(lax.rem(index, 2) == 0, 1 - at.core, at.core)
            row = choose(index // 2, [at.ring[s] for s in order])
            place([((half * 2 + core) * 4 + row) * self.block for half in range(2)], self.block)

        def second():
            give(1)
            self.total(3)
            self.late_out(0, 3)

        def fifth():
            self.land(("cross", 0, 3))
            self.early_out(0)
            self.early_out(3)

        def fourth():
            give(2)
            self.total(1)
            self.late_out(1)

        def sixth():
            give(0)
            self.total(2)
            self.late_out(4)
            self.late_next(0, 2)
            self.late_next(3, 5)

        after = {0: lambda: give(3), 2: second, 4: fourth, 5: fifth, 6: sixth}
        stepped(8, {}, step, after)
        self.total(0)
        self.land(("cross", 0, 1))
        self.early_out(1)
        self.land(("cross", 0, 2))
        self.early_out(4)
        self.early_out(2, 0)
        self.early_out(5, 3)
        for half in range(2):
            for k in (1, 4, 2, 5):
                self.land(("late", half, k))
        self.ending("late", None, 1 - at.upper, None, None)
        self.send(("last", 0, 0))
        self.land(("cross", 0, 0))
        for k in (1, 4, 2, 5):
            self.land(("early", 0, k))
        self.ending("early", dst, at.upper, lambda part: self.crossed(0, part), panel)
        self.land(("last", 0, 0))
        self.ending("late", dst, at.upper, lambda part: self.last(1, part), panel)
        self.finish()


def panel_kernel(
    low_hbm, mid_hbm, top_hbm, inv_low_hbm, inv_mid_hbm, inv_top_hbm, cpl_low_hbm, cpl_mid_hbm,
    parents_low_hbm, parents_mid_hbm,
    out_low, out_mid, out_top,
    inv_low, inv_mid, inv_top, cpl_low, cpl_mid, panel_mid, panel_top, parents_low, parents_mid,
    buf_a, buf_b, buf_c, buf_t, row_buf, z_buf, part, picked, wide,
    load, *sems,
):
    at = Place(4, 2)
    pulls = {}
    order = [
        ("low", low_hbm, rows_at(buf_a, at.row * low_hbm.shape[0], low_hbm.shape[0])),
        ("parents_low", parents_low_hbm, parents_low),
        ("parents_mid", parents_mid_hbm, parents_mid),
        ("inv_low", inv_low_hbm, inv_low),
        ("cpl_low", cpl_low_hbm, cpl_low),
        ("panel_mid", mid_hbm, panel_mid),
        ("inv_mid", inv_mid_hbm, inv_mid),
        ("cpl_mid", cpl_mid_hbm, cpl_mid),
        ("panel_top", top_hbm, panel_top),
        ("inv_top", inv_top_hbm, inv_top),
    ]
    for index, (name, src, dst) in enumerate(order):
        pulls[name] = pltpu.make_async_copy(src, dst, load.at[index])

    def need(*names):
        for name in names:
            pulls.pop(name).wait()

    for name in ("parents_low", "parents_mid", "low", "inv_low"):
        pulls[name].start()
    at.greet()
    low_sems, mid_sems, mid_sems2, top_sems, top_sems2, low_red, top_red = (
        sems[0:6], sems[6:12], sems[12:18], sems[18:24], sems[24:30], sems[30:36], sems[36:42]
    )
    need("low")
    low = Exchange(at, buf_a, 0, low_sems)
    for piece in low.pieces():
        low.begin(*piece)
    need("parents_low", "parents_mid")
    low_targets = parents_low[pl.ds(at.group, 1), :]
    mid_targets = parents_mid[pl.ds(at.group // 2, 1), :]
    spread_lanes(wide, mid_targets)
    for total in (out_low, out_mid, out_top, picked):
        total[...] = jnp.zeros_like(total)
    need("inv_low")
    for copy in pulls.values():
        copy.start()

    def user(matrix, panel, total, sign):
        def use(starts, depth):
            for start in starts:
                multiply(matrix, panel, total, start, depth, sign)

        return use

    def picker(panel):
        return lambda starts, depth: pick_add(picked, wide, panel, starts, depth)

    def placer(targets):
        return lambda starts, count: place_rows(buf_t, part, targets, starts, count)

    def begin(exchange, rows):
        for half, index in exchange.pieces():
            start, count = (half * exchange.sub + index) * exchange.count, exchange.count
            rows_at(exchange.buf, exchange.mine + start, count)[...] = rows(start, count).astype(jnp.bfloat16)
            exchange.begin(half, index)

    low.run(user(inv_low, buf_a, out_low, 1))

    need("cpl_low")
    couple_rows(cpl_low, out_low[...].astype(jnp.bfloat16), part)
    mid = Exchange(at, buf_b, 1, mid_sems)
    reduce_mid = Reduce(at, 1, buf_t, half_of(buf_c, 1), half_of(buf_c, 0), row_buf, z_buf, low_red)
    need("panel_mid")
    reduce_mid.run(placer(low_targets), panel_mid, rows_at(buf_b, mid.mine, mid.block))
    mid.begin(0)
    mid.begin(1)
    need("inv_mid")
    mid.run(user(inv_mid, buf_b, out_mid, 1))

    need("cpl_mid")
    couple_rows(cpl_mid, out_mid[...].astype(jnp.bfloat16), part)
    top = Exchange(at, buf_c, 2, top_sems)
    reduce_top = ReduceTwo(at, buf_t, half_of(buf_a, 0), half_of(buf_b, 0), row_buf, z_buf, top_red)
    need("panel_top")
    reduce_top.run(placer(mid_targets), panel_top, rows_at(buf_c, top.mine, top.block))
    top.begin(0)
    top.begin(1)
    need("inv_top")
    top.run(user(inv_top, buf_c, out_top, 1))

    back = Exchange(at, buf_t, 2, top_sems2)
    begin(back, lambda start, count: out_top[pl.ds(start, count), :])
    back.run(picker(buf_t))

    part[...] = picked[...].astype(jnp.bfloat16)
    lift = Exchange(at, buf_b, 1, mid_sems)
    begin(lift, lambda start, count: lift_rows(cpl_mid, part[...], start, count))
    spread_lanes(wide, low_targets)
    picked[...] = jnp.zeros_like(picked)
    lift.run(user(inv_mid, buf_b, out_mid, -1))

    back = Exchange(at, buf_c, 1, mid_sems2)
    begin(back, lambda start, count: out_mid[pl.ds(start, count), :])
    back.run(picker(buf_c))

    part[...] = picked[...].astype(jnp.bfloat16)
    lift = Exchange(at, buf_a, 0, low_sems)
    begin(lift, lambda start, count: lift_rows(cpl_low, part[...], start, count))
    lift.run(user(inv_low, buf_a, out_low, -1))


def settle_kernel(*refs):
    count = (len(refs) - 2) // 3
    sources, targets, held = refs[:count], refs[count : 2 * count], refs[2 * count : 3 * count]
    inward, outward = refs[3 * count :]
    pulls = [pltpu.make_async_copy(sources[i], held[i], inward.at[i]) for i in range(count)]
    pushes = [pltpu.make_async_copy(held[i], targets[i], outward.at[i]) for i in range(count)]
    for pull in pulls:
        pull.start()
    for pull, out in zip(pulls, pushes):
        pull.wait()
        out.start()
    for out in pushes:
        out.wait()


def settle(*arrays):
    count = len(arrays)
    return pl.pallas_call(
        settle_kernel,
        out_shape=tuple(jax.ShapeDtypeStruct(a.shape, a.dtype) for a in arrays),
        in_specs=[HBM_SPEC] * count,
        out_specs=(HBM_SPEC,) * count,
        scratch_shapes=[pltpu.VMEM(a.shape, a.dtype) for a in arrays] + [dma(count), dma(count)],
    )(*arrays)


def gather_sems(levels):
    units = 2 if levels >= 2 else 1
    return [dma(units, 12 if levels == 0 else 6)] * 2 + [dma(units, 8)] * 2 + [dma(2), dma(2)]


def reduce_sems(levels):
    pairs = [dma(levels, 4)] * 2
    return pairs + ([dma(3, 6)] * 2 + [dma(5)] * 2 if levels == 2 else [dma(1, 6)] * 2 + [dma(1)] * 2)


def solve_panel(
    panel_low, panel_mid, panel_top, inverse_low, inverse_mid, inverse_top, couple_low, couple_mid,
    parents_low, parents_mid,
):
    width = panel_low.shape[1]
    front, links = inverse_low.shape[2], couple_low.shape[1]

    def vmem(*shape, kind=jnp.bfloat16):
        return pltpu.VMEM(shape, kind)

    scratch = [vmem(*m.shape) for m in (inverse_low, inverse_mid, inverse_top, couple_low, couple_mid)]
    scratch += [vmem(*panel_mid.shape), vmem(*panel_top.shape)]
    scratch += [vmem(*parents.shape, kind=parents.dtype) for parents in (parents_low, parents_mid)]
    scratch += [vmem(front, width)] * 4
    scratch += [vmem(front * 3 // 8, width), vmem(3 * panel_top.shape[0], width)]
    scratch += [vmem(links, width), vmem(links, width, kind=jnp.float32)]
    scratch += [vmem(links, 128, kind=jnp.int32), dma(10)]
    scratch += gather_sems(0) + gather_sems(1) * 2 + gather_sems(2) * 2
    scratch += reduce_sems(1) + reduce_sems(2)
    solved = pl.pallas_call(
        panel_kernel,
        out_shape=tuple(
            jax.ShapeDtypeStruct(p.shape, jnp.float32) for p in (panel_low, panel_mid, panel_top)
        ),
        in_specs=[HBM_SPEC] * 10,
        out_specs=(VMEM_SPEC,) * 3,
        scratch_shapes=scratch,
        compiler_params=params(7, 63),
    )(
        panel_low, panel_mid, panel_top, inverse_low, inverse_mid, inverse_top, couple_low, couple_mid,
        parents_low, parents_mid,
    )
    return settle(*solved)


def on_device(
    n,
    panel_low,
    panel_mid,
    panel_top,
    inverse_low,
    inverse_mid,
    inverse_top,
    couple_low,
    couple_mid,
    parents_low,
    parents_mid,
):
    if n == 4:
        return solve_panel(
            panel_low, panel_mid, panel_top, inverse_low, inverse_mid, inverse_top, couple_low, couple_mid,
            parents_low, parents_mid,
        )
    group = lax.axis_index("grp")
    low_targets = lax.dynamic_index_in_dim(parents_low, group, 0, keepdims=False)
    mid_targets = lax.dynamic_index_in_dim(parents_mid, group // 2, 0, keepdims=False)
    low_y = gather_solve(panel_low, inverse_low, n, 0, 0)
    term = spread_rows(complex_product(couple_low, low_y.astype(jnp.bfloat16)), low_targets)
    mid_y = reduce_solve(term, panel_mid, inverse_mid, n, 1, 1)
    term = spread_rows(complex_product(couple_mid, mid_y.astype(jnp.bfloat16)), mid_targets)
    top_x = reduce_solve(term, panel_top, inverse_top, n, 2, 2)
    top_full = gather(top_x.astype(jnp.bfloat16), n, 2, 3)
    lift = transposed_product(couple_mid, pick_rows(top_full, mid_targets)).astype(jnp.bfloat16)
    mid_x = mid_y - gather_solve(lift, inverse_mid, n, 1, 4)
    mid_full = gather(mid_x.astype(jnp.bfloat16), n, 1, 5)
    lift = transposed_product(couple_low, pick_rows(mid_full, low_targets)).astype(jnp.bfloat16)
    low_x = low_y - gather_solve(lift, inverse_low, n, 0, 6)
    return (low_x, mid_x, top_x)


def solution(mesh):
    placed = (
        P(("grp", "row"), None),
        P(("grp", "row"), None),
        P(("grp", "row"), None),
        P(None, ("grp", "row"), None),
        P(None, ("grp", "row"), None),
        P(None, ("grp", "row"), None),
        P(None, None, ("grp", "row")),
        P(None, None, ("grp", "row")),
        P(),
        P(),
    )
    return jax.shard_map(
        functools.partial(on_device, mesh.shape["row"]),
        mesh=mesh,
        in_specs=placed,
        out_specs=(P(("grp", "row"), None), P(("grp", "row"), None), P(("grp", "row"), None)),
        check_vma=False,
    )
```

```python
import functools
import math

import jax
import jax.numpy as jnp
from jax import lax
from jax.experimental import pallas as pl
from jax.experimental.pallas import tpu as pltpu
from jax.sharding import PartitionSpec as P

F = 4096
MESH = pl.DeviceIdType.MESH


def complex_product(matrix, panel):
    width = panel.shape[1] // 2
    real_term = jnp.dot(matrix[0], panel, preferred_element_type=jnp.float32)
    imag_term = jnp.dot(matrix[1], panel, preferred_element_type=jnp.float32)
    return real_term + jnp.concatenate([-imag_term[:, width:], imag_term[:, :width]], axis=1)


def transposed_product(matrix, panel):
    width = panel.shape[1] // 2
    contract = (((0,), (0,)), ((), ()))
    real_term = lax.dot_general(matrix[0], panel, contract, preferred_element_type=jnp.float32)
    imag_term = lax.dot_general(matrix[1], panel, contract, preferred_element_type=jnp.float32)
    return real_term + jnp.concatenate([-imag_term[:, width:], imag_term[:, :width]], axis=1)


class Place:
    def __init__(self, n, levels):
        self.n = n
        self.levels = levels
        self.square = n == 4
        self.group = lax.axis_index("grp")
        self.row = lax.axis_index("row")
        self.core = lax.rem(self.group, 2)
        self.upper = lax.rem(self.group // 2, 2)
        self.partner = (self.group + 1 - 2 * self.core, self.row)
        self.across = (self.group + 2 - 4 * self.upper, self.row)
        self.unit = lax.rem(self.group, 2**levels)
        if self.square:
            side = self.row + 1 - 2 * lax.rem(self.row, 2)
            over = self.row + 2 - 4 * (self.row // 2)
            self.ring = [self.row, side, over, 3 - self.row]
            self.side = (self.group, side)
            self.over = (self.group, over)

    def ahead(self, step):
        return self.ring[step] if self.square else lax.rem(self.row + step, self.n)

    def behind(self, step):
        return self.ring[step] if self.square else lax.rem(self.row + self.n - step, self.n)

    def greet(self):
        barrier = pltpu.get_barrier_semaphore()
        if self.square:
            peers = [self.side, self.over]
        else:
            peers = [(self.group, self.ahead(s)) for s in range(1, self.n)]
        if self.levels >= 1:
            peers.append(self.partner)
        if self.levels >= 2:
            peers.append(self.across)
        for peer in peers:
            pl.semaphore_signal(barrier, inc=1, device_id=peer, device_id_type=MESH)
        pl.semaphore_wait(barrier, len(peers))


def push(src, dst, send, recv, peer):
    return pltpu.make_async_remote_copy(
        src_ref=src, dst_ref=dst, send_sem=send, recv_sem=recv, device_id=peer, device_id_type=MESH
    )


def half_of(ref, index):
    rows = ref.shape[0] // 2
    return ref.at[pl.ds(index * rows, rows)]


def spread(at, out, sems, use):
    n, levels = at.n, at.levels
    row_send, row_recv, pair_send, pair_recv, z_send, z_recv = sems
    near = at.unit
    started = []

    def go(src, send, recv, peer):
        copy = push(src, src, send, recv, peer)
        copy.start()
        started.append(copy)

    def landed(ref, send, recv, peer):
        push(ref, ref, send, recv, peer).wait_recv()

    def row_copy(act, which, k, slot, half, peer):
        act(half_of(out.at[slot], half), row_send.at[which, k], row_recv.at[which, k], peer)

    def to_rows(which, unit):
        mine = unit * n + at.row
        if at.square:
            row_copy(go, which, 0, mine, 0, at.side)
            row_copy(go, which, 1, mine, 1, at.over)
            row_copy(go, which, 2, mine, 1, at.side)
            row_copy(go, which, 3, mine, 0, at.over)
            return
        for s in range(1, n):
            go(out.at[mine], row_send.at[which, s], row_recv.at[which, s], (at.group, at.ahead(s)))

    def forward(which, unit):
        if at.square:
            side, over = unit * n + at.ring[1], unit * n + at.ring[2]
            row_copy(landed, which, 0, side, 0, at.side)
            row_copy(go, which, 4, side, 0, at.over)
            row_copy(landed, which, 1, over, 1, at.over)
            row_copy(go, which, 5, over, 1, at.side)

    def await_row(which, unit, s):
        slot = unit * n + at.behind(s)
        if not at.square:
            peer = (at.group, at.behind(s))
            landed(out.at[slot], row_send.at[which, s], row_recv.at[which, s], peer)
        elif s == 1:
            row_copy(landed, which, 2, slot, 1, at.side)
        elif s == 2:
            row_copy(landed, which, 3, slot, 0, at.over)
        else:
            row_copy(landed, which, 4, slot, 0, at.over)
            row_copy(landed, which, 5, slot, 1, at.side)

    def to_pair(which, s, unit):
        src = out.at[unit * n + at.behind(s)]
        go(src, pair_send.at[which, s], pair_recv.at[which, s], at.partner)

    def await_pair(which, s, unit):
        slot = (unit + 1 - 2 * at.core) * n + at.behind(s)
        landed(out.at[slot], pair_send.at[which, s], pair_recv.at[which, s], at.partner)
        use(slot)

    units = [near]
    if levels >= 2:
        units.append(lax.rem(near + 2, 4))
        go(out.at[near * n + at.row], z_send.at[0], z_recv.at[0], at.across)
    to_rows(0, near)
    if levels >= 1:
        to_pair(0, 0, near)
    if levels >= 2:
        landed(out.at[units[1] * n + at.row], z_send.at[0], z_recv.at[0], at.across)
        to_rows(1, units[1])
        to_pair(1, 0, units[1])
    use(near * n + at.row)
    if levels >= 2:
        use(units[1] * n + at.row)
    for which, unit in enumerate(units):
        forward(which, unit)
    for s in range(1, n):
        for which, unit in enumerate(units):
            await_row(which, unit, s)
            if levels >= 1:
                to_pair(which, s, unit)
                await_pair(which, s - 1, unit)
            use(unit * n + at.behind(s))
    if levels >= 1:
        for which, unit in enumerate(units):
            await_pair(which, n - 1, unit)
    for copy in started:
        copy.wait_send()


def solver(n, out, inverse_hbm, inverse, turned, total, sem):
    count, block, width = out.shape
    rows = inverse.shape[1]
    tile = min(rows, 256)
    whole = block % 128 == 0
    together = 1 if whole else turned.shape[0] // block
    copy = pltpu.make_async_copy(inverse_hbm, inverse, sem)
    copy.start()
    waiting = [copy]

    def multiply(slot, first):
        panel = out[slot] if whole else out[pl.ds(slot, together)].reshape(turned.shape)
        half = width // 2
        turned[:, :half] = -panel[:, half:]
        turned[:, half:] = panel[:, :half]
        span_columns = turned.shape[0]
        columns = pl.ds(pl.multiple_of(slot // together * span_columns, span_columns), span_columns)

        def body(index, carry):
            span = pl.ds(pl.multiple_of(index * tile, tile), tile)
            block_now = out[slot] if whole else panel
            real = jnp.dot(inverse[0, span, columns], block_now, preferred_element_type=jnp.float32)
            imag = jnp.dot(inverse[1, span, columns], turned[...], preferred_element_type=jnp.float32)
            if first:
                total[span, :] = real + imag
            else:
                total[span, :] = total[span, :] + (real + imag)
            return carry

        lax.fori_loop(0, rows // tile, body, 0)

    def use(slot):
        if whole:
            first = bool(waiting)
            if first:
                waiting.pop().wait()
            multiply(slot, first)

    def rest():
        if not whole:
            waiting.pop().wait()
            for slot in range(0, count, together):
                multiply(slot, slot == 0)

    return use, rest


def gather_kernel(n, levels, own, full, *sems):
    at = Place(n, levels)
    at.greet()
    full[at.unit * n + at.row] = own[...]
    spread(at, full, sems, lambda slot: None)


def gather_solve_kernel(n, levels, own, inverse_hbm, total, full, inverse, turned, sem, *sems):
    at = Place(n, levels)
    use, rest = solver(n, full, inverse_hbm, inverse, turned, total, sem)
    at.greet()
    full[at.unit * n + at.row] = own[...]
    spread(at, full, sems, use)
    rest()


def add_rows(out_ref, terms, panel=None):
    rows = out_ref.shape[0]
    step = min(rows, 64)

    def body(index, carry):
        span = pl.ds(pl.multiple_of(index * step, step), step)
        total = terms[0][span, :].astype(jnp.float32)
        for term in terms[1:]:
            total = total + term[span, :].astype(jnp.float32)
        if panel is not None:
            total = panel[span, :].astype(jnp.float32) - total
        out_ref[span, :] = total.astype(out_ref.dtype)
        return carry

    lax.fori_loop(0, rows // step, body, 0)


def reduce_solve_kernel(
    n, levels, term, panel, inverse_hbm, total, full, inverse, turned, near_buf, stage, row_buf, z_buf, sem, *sems
):
    at = Place(n, levels)
    halves = 2 ** (levels - 1)
    spread_sems = sems[:6]
    pair_send, pair_recv, row_send, row_recv, z_send, z_recv = sems[6:]
    use, finish_solve = solver(n, full, inverse_hbm, inverse, turned, total, sem)
    at.greet()
    started = []

    def go(src, dst, send, recv, peer):
        copy = push(src, dst, send, recv, peer)
        copy.start()
        started.append(copy)

    def landed(ref, send, recv, peer):
        push(ref, ref, send, recv, peer).wait_recv()

    order = [3, 1, 2, 0] if at.square else list(range(1, n)) + [0]
    for s in order:
        for half in range(halves):
            src = term.at[(half * 2 + 1 - at.core) * n + at.ahead(s)]
            go(src, near_buf.at[half, s], pair_send.at[half, s], pair_recv.at[half, s], at.partner)

    def own_term(half, s):
        return term.at[(half * 2 + at.core) * n + at.ahead(s)]

    def await_pair(half, s):
        landed(near_buf.at[half, s], pair_send.at[half, s], pair_recv.at[half, s], at.partner)

    def row_copy(half, k, src, peer):
        go(src, row_buf.at[half, k], row_send.at[half, k], row_recv.at[half, k], peer)

    def await_row(half, k, peer):
        landed(row_buf.at[half, k], row_send.at[half, k], row_recv.at[half, k], peer)

    if at.square:
        for half in range(halves):
            await_pair(half, 3)
            add_rows(stage.at[half, 3], [own_term(half, 3), near_buf.at[half, 3]])
            row_copy(half, 0, half_of(stage.at[half, 3], 0), at.side)
            row_copy(half, 3, half_of(stage.at[half, 3], 1), at.over)
        for half in range(halves):
            await_pair(half, 1)
            first = half_of(stage.at[half, 1], 0)
            add_rows(first, [half_of(own_term(half, 1), 0), half_of(near_buf.at[half, 1], 0)])
            row_copy(half, 1, first, at.side)
            await_pair(half, 2)
            second = half_of(stage.at[half, 2], 1)
            add_rows(second, [half_of(own_term(half, 2), 1), half_of(near_buf.at[half, 2], 1)])
            row_copy(half, 4, second, at.over)
        for half in range(halves):
            await_row(half, 0, at.side)
            first = half_of(stage.at[half, 2], 0)
            near = half_of(near_buf.at[half, 2], 0)
            add_rows(first, [half_of(own_term(half, 2), 0), near, row_buf.at[half, 0]])
            row_copy(half, 2, first, at.over)
            await_row(half, 3, at.over)
            second = half_of(stage.at[half, 1], 1)
            near = half_of(near_buf.at[half, 1], 1)
            add_rows(second, [half_of(own_term(half, 1), 1), near, row_buf.at[half, 3]])
            row_copy(half, 5, second, at.side)
        for half in range(halves):
            await_pair(half, 0)
            await_row(half, 1, at.side)
            await_row(half, 4, at.over)
            await_row(half, 2, at.over)
            await_row(half, 5, at.side)
    else:
        for s in range(1, n):
            for half in range(halves):
                await_pair(half, s)
                add_rows(stage.at[half, s], [own_term(half, s), near_buf.at[half, s]])
                row_copy(half, s, stage.at[half, s], (at.group, at.ahead(s)))
        for half in range(halves):
            await_pair(half, 0)
            for s in range(1, n):
                await_row(half, s, (at.group, at.behind(s)))

    def finish(dst, half, extra, base):
        own, near = own_term(half, 0), near_buf.at[half, 0]
        if not at.square:
            rest = [row_buf.at[half, s] for s in range(1, n)]
            add_rows(dst, [own, near] + rest + extra, base)
            return
        for part in range(2):
            rest = [row_buf.at[half, 1 + 3 * part], row_buf.at[half, 2 + 3 * part]]
            rest = rest + [half_of(ref, part) for ref in extra]
            terms = [half_of(own, part), half_of(near, part)] + rest
            add_rows(half_of(dst, part), terms, None if base is None else half_of(base, part))

    slot = at.unit * n + at.row
    if levels == 1:
        finish(full.at[slot], 0, [], panel)
    else:
        finish(z_buf.at[0], 1 - at.upper, [], None)
        go(z_buf.at[0], z_buf.at[1], z_send.at[0], z_recv.at[0], at.across)
        landed(z_buf.at[1], z_send.at[0], z_recv.at[0], at.across)
        finish(full.at[slot], at.upper, [z_buf.at[1]], panel)
    spread(at, full, spread_sems, use)
    finish_solve()
    for copy in started:
        copy.wait_send()


def dma(*shape):
    return pltpu.SemaphoreType.DMA(shape)


VMEM_SPEC = pl.BlockSpec(memory_space=pltpu.VMEM)
HBM_SPEC = pl.BlockSpec(memory_space=pltpu.HBM)


def spread_scratch(n):
    k = max(n, 6)
    return [dma(2, k), dma(2, k), dma(2, n), dma(2, n), dma(1), dma(1)]


def params(ident, mebibytes):
    return pltpu.CompilerParams(
        collective_id=ident, has_side_effects=True, vmem_limit_bytes=mebibytes << 20
    )


def gather(own, n, levels, ident):
    block, width = own.shape
    count = 2**levels * n
    full = pl.pallas_call(
        functools.partial(gather_kernel, n, levels),
        out_shape=jax.ShapeDtypeStruct((count, block, width), own.dtype),
        in_specs=[VMEM_SPEC],
        out_specs=VMEM_SPEC,
        scratch_shapes=spread_scratch(n),
        compiler_params=params(ident, 16),
    )(own)
    return full.reshape(count * block, width)


def solve_scratch(inverse, block, width, count):
    return [
        pltpu.VMEM((count, block, width), jnp.bfloat16),
        pltpu.VMEM(inverse.shape, inverse.dtype),
        pltpu.VMEM((block if block % 128 == 0 else 512, width), jnp.bfloat16),
    ]


def gather_solve(own, inverse, n, levels, ident):
    block, width = own.shape
    return pl.pallas_call(
        functools.partial(gather_solve_kernel, n, levels),
        out_shape=jax.ShapeDtypeStruct((inverse.shape[1], width), jnp.float32),
        in_specs=[VMEM_SPEC, HBM_SPEC],
        out_specs=VMEM_SPEC,
        scratch_shapes=solve_scratch(inverse, block, width, 2**levels * n)
        + [pltpu.SemaphoreType.DMA]
        + spread_scratch(n),
        compiler_params=params(ident, 32),
    )(own, inverse)


def reduce_solve(term, panel, inverse, n, levels, ident):
    block, width = panel.shape
    count = 2**levels * n
    halves = 2 ** (levels - 1)
    whole = pltpu.VMEM((halves, n, block, width), jnp.bfloat16)
    if n == 4:
        pieces, k = pltpu.VMEM((halves, 6, block // 2, width), jnp.bfloat16), 6
    else:
        pieces, k = whole, n
    return pl.pallas_call(
        functools.partial(reduce_solve_kernel, n, levels),
        out_shape=jax.ShapeDtypeStruct((inverse.shape[1], width), jnp.float32),
        in_specs=[VMEM_SPEC, VMEM_SPEC, HBM_SPEC],
        out_specs=VMEM_SPEC,
        scratch_shapes=solve_scratch(inverse, block, width, count)
        + [whole, whole, pieces, pltpu.VMEM((2, block, width), jnp.bfloat16)]
        + [pltpu.SemaphoreType.DMA]
        + spread_scratch(n)
        + [dma(halves, n), dma(halves, n), dma(halves, k), dma(halves, k), dma(1), dma(1)],
        compiler_params=params(ident, 32),
    )(term.reshape(count, block, width), panel, inverse)


def spread_kernel(tile, targets, rows, out):
    index = lax.broadcasted_iota(jnp.int32, (tile, 1), 0) + pl.program_id(0) * tile
    marks = (index == targets[...]).astype(jnp.float32).astype(jnp.bfloat16)
    out[...] = jnp.dot(marks, rows[...], preferred_element_type=jnp.float32).astype(out.dtype)


def spread_rows(partial_rows, targets):
    count, width = partial_rows.shape
    tile = F // 4
    return pl.pallas_call(
        functools.partial(spread_kernel, tile),
        grid=(F // tile,),
        in_specs=[
            pl.BlockSpec((1, count), lambda i: (0, 0)),
            pl.BlockSpec((count, width), lambda i: (0, 0)),
        ],
        out_specs=pl.BlockSpec((tile, width), lambda i: (i, 0)),
        out_shape=jax.ShapeDtypeStruct((F, width), jnp.bfloat16),
        compiler_params=pltpu.CompilerParams(vmem_limit_bytes=32 << 20),
    )(targets[None, :], partial_rows.astype(jnp.bfloat16))


def pick_rows(panel, targets):
    marks = (targets[:, None] == lax.broadcasted_iota(jnp.int32, (1, F), 1)).astype(jnp.bfloat16)
    return jnp.dot(marks, panel, preferred_element_type=jnp.float32).astype(jnp.bfloat16)


def dot32(left, right):
    return jnp.dot(left, right, preferred_element_type=jnp.float32)


def turn(product):
    half, width = product.shape[0] // 2, product.shape[1] // 2
    real, imag = product[:half], product[half:]
    return real + jnp.concatenate([-imag[:, width:], imag[:, :width]], axis=1)


def rows_at(ref, start, count):
    return ref.at[pl.ds(pl.multiple_of(start, math.gcd(count, 256)), count)]


def multiply(matrix, panel, total, start, depth, sign):
    rows = matrix.shape[1]
    tile = min(rows, 512)
    span = pl.ds(pl.multiple_of(start, depth), depth)
    block = panel[span, :]
    for base in range(0, rows, tile):
        part = pl.ds(base, tile)
        left = matrix[:, part, span].reshape(2 * tile, depth)
        product = turn(dot32(left, block))
        total[part, :] = total[part, :] + product if sign > 0 else total[part, :] - product


def choose(index, values):
    out = values[-1]
    for k in range(len(values) - 2, -1, -1):
        out = jnp.where(index == k, values[k], out)
    return out


def stepped(count, before, step, after):
    def body(index, carry):
        for k, event in before.items():
            pl.when(index == k)(event)
        step(index)
        for k, event in after.items():
            pl.when(index == k)(event)
        return carry

    lax.fori_loop(0, count, body, 0)


def couple_rows(matrix, panel, out):
    tile = 1024
    for base in range(0, matrix.shape[1], tile):
        part = pl.ds(base, tile)
        left = matrix[:, part, :].reshape(2 * tile, matrix.shape[2])
        out[part, :] = turn(dot32(left, panel)).astype(out.dtype)


def lift_rows(matrix, panel, start, count):
    columns = pl.ds(start, count)
    contract = (((0,), (0,)), ((), ()))
    real = lax.dot_general(matrix[0, :, columns], panel, contract, preferred_element_type=jnp.float32)
    imag = lax.dot_general(matrix[1, :, columns], panel, contract, preferred_element_type=jnp.float32)
    width = panel.shape[1] // 2
    return real + jnp.concatenate([-imag[:, width:], imag[:, :width]], axis=1)


def place_rows(term, part, targets, starts, count):
    iota = lax.broadcasted_iota(jnp.int32, (count, 1), 0)
    marks = [(iota + start == targets).astype(jnp.float32).astype(jnp.bfloat16) for start in starts]
    placed = dot32(jnp.concatenate(marks, axis=0), part[...])
    for index, start in enumerate(starts):
        rows_at(term, start, count)[...] = placed[index * count : (index + 1) * count].astype(term.dtype)


def spread_lanes(wide, targets):
    for base in range(0, wide.shape[0], 128):
        square = jnp.broadcast_to(targets[:, base : base + 128], (128, 128))
        wide[pl.ds(base, 128), :] = square.T


def pick_add(total, wide, panel, starts, depth):
    blocks = [panel[pl.ds(pl.multiple_of(start, depth), depth), :] for start in starts]
    block = jnp.concatenate(blocks, axis=0) if len(blocks) > 1 else blocks[0]
    lanes = lax.broadcasted_iota(jnp.int32, (1, 128), 1)
    tile = 1024
    for base in range(0, wide.shape[0], tile):
        part = pl.ds(base, tile)
        wanted = wide[part, :]
        marks = []
        for start in starts:
            for shift in range(0, depth, 128):
                marks.append((lanes + (start + shift) == wanted).astype(jnp.float32).astype(jnp.bfloat16))
        total[part, :] = total[part, :] + dot32(jnp.concatenate(marks, axis=1), block)


def add_all(out, terms, base=None):
    total = terms[0][...].astype(jnp.float32)
    for term in terms[1:]:
        total = total + term[...].astype(jnp.float32)
    if base is not None:
        total = base[...].astype(jnp.float32) - total
    out[...] = total.astype(out.dtype)


class Sender:
    def __init__(self):
        self.log = {}

    def send(self, key):
        self.copy(*key).start()
        self.log[key] = True

    def land(self, key):
        self.copy(*key, arriving=True).wait_recv()

    def sent(self, *keys):
        for key in keys:
            del self.log[key]
            self.copy(*key).wait_send()

    def finish(self):
        self.sent(*list(self.log))


class Exchange(Sender):
    def __init__(self, at, buf, levels, sems, source=None):
        super().__init__()
        self.at, self.buf, self.levels, self.sems, self.source = at, buf, levels, sems, source
        self.block = buf.shape[0] // (4 * 2**levels)
        self.sub = 2 if levels == 0 else 1
        self.count = self.block // (2 * self.sub)
        near = lax.rem(at.group, 2**levels)
        self.units = [near]
        if levels >= 2:
            self.units.append(lax.rem(near + 2, 4))
        self.mine = self.start_of(near, 0)

    def start_of(self, unit, s):
        return (unit * 4 + self.at.ring[s]) * self.block

    def copy(self, kind, which, a, b, arriving=False):
        row_send, row_recv, pair_send, pair_recv, z_send, z_recv = self.sems
        at, unit, index = self.at, self.units[which], 0
        if kind == "row":
            link, stage, index = a, b // self.sub, b % self.sub
            outward = [(0, link), (0, 1 - link), (2 - link, 1 - link)]
            inward = [(1 + link, link), (1 + link, 1 - link), (3, 1 - link)]
            s, half = (inward if arriving else outward)[stage]
            k, peer = link * 3 * self.sub + b, at.over if link else at.side
            send, recv = row_send.at[which, k], row_recv.at[which, k]
        elif kind == "pair":
            s, half = a, b
            send, recv, peer = pair_send.at[which, 2 * s + half], pair_recv.at[which, 2 * s + half], at.partner
            unit = unit + 1 - 2 * at.core if arriving else unit
        else:
            s, half = 0, b
            send, recv, peer = z_send.at[half], z_recv.at[half], at.across
            unit = self.units[1] if arriving else self.units[0]
        shift = (half * self.sub + index) * self.count
        ref = rows_at(self.buf, self.start_of(unit, s) + shift, self.count)
        src = ref
        if self.source is not None and s == 0 and not arriving:
            src = self.source.at[pl.ds(shift, self.count)]
        return push(src, ref, send, recv, peer)

    def pieces(self):
        return [(half, index) for index in range(self.sub) for half in range(2)]

    def begin(self, half, index=0):
        self.send(("row", 0, half, index))
        if self.levels == 0:
            self.send(("row", 0, 1 - half, self.sub + index))
        if self.levels >= 2:
            self.send(("z", 0, 0, half))
        if self.levels >= 1:
            self.send(("pair", 0, 0, half))

    def arrive(self, which, link, stage, index=0):
        self.land(("row", which, link, stage * self.sub + index))
        if stage == 0:
            self.send(("row", which, 1 - link, 2 * self.sub + index))
        if self.levels >= 1:
            s, half = [(1 + link, link), (1 + link, 1 - link), (3, 1 - link)][stage]
            self.send(("pair", which, s, half))

    def both(self, which, stage):
        for link, index in self.pieces():
            self.arrive(which, link, stage, index)

    def second(self, which):
        for link, index in self.pieces():
            self.sent(("row", which, link, index))
            self.send(("row", which, link, self.sub + index))

    def await_pair(self, which, *rows):
        for s in rows:
            for half in range(2):
                self.land(("pair", which, s, half))

    def z_first(self):
        for half in range(2):
            self.land(("z", 0, 0, half))
            self.send(("row", 1, half, 0))
            self.send(("pair", 1, 0, half))

    def run(self, use):
        def block(which, other, s):
            return self.start_of(self.units[which] + (1 - 2 * self.at.core) * other, s)

        def then(*events):
            def event():
                for call, *arguments in events:
                    call(*arguments)

            return event

        if self.levels == 0:
            order = [(0, 0), (0, 1), (0, 2), (0, 3), (1, 0), (2, 2), (1, 1), (2, 3)]
            order += [(1, 2), (2, 0), (1, 3), (2, 1), (3, 0), (3, 2), (3, 1), (3, 3)]
            starts = [[block(0, 0, s) + piece * self.count for s, piece in order]]
            depth = self.count
            before = {4: then((self.both, 0, 0)), 8: then((self.both, 0, 1))}
            for step, (link, index) in ((12, (1, 0)), (13, (0, 0)), (14, (1, 1)), (15, (0, 1))):
                before[step] = then((self.arrive, 0, link, 2, index))
        elif self.levels == 1:
            halves = [
                [(0, 0, 0), (1, 0, 0), (0, 1, 0), (1, 1, 0), (0, 1, 1), (1, 1, 1), (0, 3, 0), (1, 3, 0)],
                [(0, 0, 1), (1, 0, 1), (0, 2, 1), (1, 2, 1), (0, 2, 0), (1, 2, 0), (0, 3, 1), (1, 3, 1)],
            ]
            starts = [[block(0, other, s) + half * self.count for other, s, half in line] for line in halves]
            depth = self.count
            before = {
                1: then((self.await_pair, 0, 0)),
                2: then((self.second, 0), (self.both, 0, 0)),
                3: then((self.land, ("pair", 0, 1, 0)), (self.land, ("pair", 0, 2, 1))),
                4: then((self.both, 0, 1)),
                5: then((self.land, ("pair", 0, 1, 1)), (self.land, ("pair", 0, 2, 0))),
                6: then((self.both, 0, 2)),
                7: then((self.await_pair, 0, 3)),
            }
        else:
            starts = [
                [block(*b) for b in line]
                for line in (
                    [(0, 0, 0), (0, 0, 1), (0, 1, 1), (1, 0, 0), (0, 0, 3), (1, 0, 1), (1, 1, 1), (1, 0, 3)],
                    [(0, 1, 0), (0, 0, 2), (0, 1, 2), (1, 1, 0), (0, 1, 3), (1, 0, 2), (1, 1, 2), (1, 1, 3)],
                )
            ]
            depth = self.block
            before = {
                0: then((self.await_pair, 0, 0)),
                1: then((self.second, 0), (self.both, 0, 0), (self.z_first,), (self.both, 0, 1)),
                2: then((self.await_pair, 0, 1, 2)),
                3: then((self.second, 1), (self.both, 0, 2), (self.await_pair, 1, 0)),
                4: then((self.both, 1, 0), (self.await_pair, 0, 3)),
                5: then((self.both, 1, 1)),
                6: then((self.both, 1, 2), (self.await_pair, 1, 1, 2)),
                7: then((self.await_pair, 1, 3)),
            }
        count = len(starts[0])
        stepped(count, before, lambda i: use([choose(i, line) for line in starts], depth), {})
        self.finish()


class Reduce(Sender):
    def __init__(self, at, levels, term, near, stage, row_buf, z_buf, sems):
        super().__init__()
        self.at, self.levels, self.term, self.sems = at, levels, term, sems
        self.halves = 2 ** (levels - 1)
        self.block = term.shape[0] // (8 * self.halves)
        self.near_buf, self.stage_buf, self.row_buf, self.z_buf = near, stage, row_buf, z_buf

    def start_of(self, half, core, s):
        return ((half * 2 + core) * 4 + self.at.ring[s]) * self.block

    def own(self, half, s):
        return rows_at(self.term, self.start_of(half, self.at.core, s), self.block)

    def near(self, half, s):
        return rows_at(self.near_buf, (half * 4 + s) * self.block, self.block)

    def stage(self, half, s):
        return rows_at(self.stage_buf, (half * 4 + s) * self.block, self.block)

    def arrived(self, half, k):
        rows = self.block // 2
        return rows_at(self.row_buf, (half * 6 + k) * rows, rows)

    def copy(self, kind, half, k, arriving=False):
        pair_send, pair_recv, row_send, row_recv, z_send, z_recv = self.sems
        at = self.at
        if kind == "pair":
            away = rows_at(self.term, self.start_of(half, 1 - at.core, k), self.block)
            near = self.near(half, k)
            return push(near if arriving else away, near, pair_send.at[half, k], pair_recv.at[half, k], at.partner)
        if kind == "row":
            peer = at.side if k in (0, 1, 5) else at.over
            s, part = [(3, 0), (1, 0), (2, 0), (3, 1), (2, 1), (1, 1)][k]
            src = self.arrived(half, k) if arriving else half_of(self.stage(half, s), part)
            return push(src, self.arrived(half, k), row_send.at[half, k], row_recv.at[half, k], peer)
        mine, theirs = half_of(self.z_buf, 0), half_of(self.z_buf, 1)
        return push(theirs if arriving else mine, theirs, z_send.at[0], z_recv.at[0], at.across)

    def await_pair(self, s):
        for half in range(self.halves):
            self.land(("pair", half, s))

    def add_half(self, half, k, extra):
        s, part = [(3, 0), (1, 0), (2, 0), (3, 1), (2, 1), (1, 1)][k]
        out = half_of(self.stage(half, s), part)
        add_all(out, [half_of(self.own(half, s), part), half_of(self.near(half, s), part)] + extra)
        self.send(("row", half, k))

    def add_halves(self, s, *ks):
        self.await_pair(s)
        for half in range(self.halves):
            for k in ks:
                self.add_half(half, k, [])

    def add_final(self, out, half, extra, base):
        for part in range(2):
            terms = [half_of(self.own(half, 0), part), half_of(self.near(half, 0), part)]
            terms += [self.arrived(half, 1 + 3 * part), self.arrived(half, 2 + 3 * part)]
            terms += [half_of(ref, part) for ref in extra]
            add_all(half_of(out, part), terms, None if base is None else half_of(base, part))

    def run(self, place, panel, dst):
        halves, at = range(self.halves), self.at
        order = (3, 1, 2, 0)

        def give(s):
            for half in halves:
                self.send(("pair", half, s))

        def step(index):
            core = jnp.where(lax.rem(index, 2) == 0, 1 - at.core, at.core)
            row = choose(index // 2, [at.ring[s] for s in order])
            place([((half * 2 + core) * 4 + row) * self.block for half in halves], self.block)

        def then(*events):
            def event():
                for one in events:
                    one()

            return event

        after = {
            0: lambda: give(3),
            2: then(lambda: give(1), lambda: self.add_halves(3, 0, 3)),
            4: then(lambda: give(2), lambda: self.add_halves(1, 1)),
            6: then(lambda: give(0), lambda: self.add_halves(2, 4)),
        }
        stepped(8, {}, step, after)
        for half in halves:
            self.land(("row", half, 0))
            self.add_half(half, 2, [self.arrived(half, 0)])
            self.land(("row", half, 3))
            self.add_half(half, 5, [self.arrived(half, 3)])
        self.await_pair(0)
        for half in halves:
            for k in (1, 4, 2, 5):
                self.land(("row", half, k))
        self.add_final(dst, 0, [], panel)
        self.finish()


STEPS = [(3, 0), (1, 0), (2, 0), (3, 1), (2, 1), (1, 1)]


class ReduceTwo(Sender):
    def __init__(self, at, term, near, stage, row_buf, z_buf, sems):
        super().__init__()
        self.at, self.term, self.sems = at, term, sems
        self.block = term.shape[0] // 16
        self.early = self.block * 5 // 8
        self.late = self.block - self.early
        self.near_buf, self.stage_buf, self.row_buf, self.z_buf = near, stage, row_buf, z_buf

    def start_of(self, half, core, s):
        return ((half * 2 + core) * 4 + self.at.ring[s]) * self.block

    def own(self, half, s):
        return rows_at(self.term, self.start_of(half, self.at.core, s), self.block)

    def near(self, half, s):
        return rows_at(self.near_buf, (half * 4 + s) * self.block, self.block)

    def window(self, kind, part=None):
        start, rows = (0, self.early) if kind == "early" else (self.early, self.late)
        return (start, rows) if part is None else (start + part * (rows // 2), rows // 2)

    def stage(self, kind, half, s, part=None):
        start, rows = self.window(kind, part)
        return rows_at(self.stage_buf, (half * 4 + s) * self.block + start, rows)

    def arrived(self, kind, half, k):
        rows = self.window(kind, 0)[1]
        if kind == "early":
            return rows_at(self.row_buf, self.late * 6 + k * rows, rows)
        return rows_at(self.row_buf, (half * 6 + k) * rows, rows)

    def crossed(self, s, part=None):
        start, rows = self.window("early", part)
        return rows_at(self.z_buf, s * self.early + start, rows)

    def last(self, index, part=None):
        rows = self.late if part is None else self.late // 2
        return rows_at(self.z_buf, 4 * self.early + index * self.late + (part or 0) * rows, rows)

    def copy(self, kind, half, k, arriving=False):
        pair_send, pair_recv, row_send, row_recv, z_send, z_recv = self.sems
        at = self.at
        if kind == "pair":
            away = rows_at(self.term, self.start_of(half, 1 - at.core, k), self.block)
            near = self.near(half, k)
            return push(near if arriving else away, near, pair_send.at[half, k], pair_recv.at[half, k], at.partner)
        if kind == "cross":
            src = self.crossed(k) if arriving else self.stage("early", 1 - at.upper, k)
            return push(src, self.crossed(k), z_send.at[k], z_recv.at[k], at.across)
        if kind == "last":
            return push(self.last(1 if arriving else 0), self.last(1), z_send.at[4], z_recv.at[4], at.across)
        peer = at.side if k in (0, 1, 5) else at.over
        s, part = STEPS[k]
        dst = self.arrived(kind, half, k)
        src = dst if arriving else self.stage(kind, at.upper if kind == "early" else half, s, part)
        group = 2 if kind == "early" else half
        return push(src, dst, row_send.at[group, k], row_recv.at[group, k], peer)

    def total(self, s):
        for half in range(2):
            self.land(("pair", half, s))
            out = rows_at(self.stage_buf, (half * 4 + s) * self.block, self.block)
            add_all(out, [self.own(half, s), self.near(half, s)])
        self.send(("cross", 0, s))

    def late_out(self, *ks):
        for half in range(2):
            for k in ks:
                self.send(("late", half, k))

    def late_next(self, before, k):
        s, part = STEPS[k]
        for half in range(2):
            self.land(("late", half, before))
            out = self.stage("late", half, s, part)
            add_all(out, [out, self.arrived("late", half, before)])
            self.send(("late", half, k))

    def early_out(self, k, before=None):
        s, part = STEPS[k]
        out = self.stage("early", self.at.upper, s, part)
        terms = [out, self.crossed(s, part)]
        if before is not None:
            self.land(("early", 0, before))
            terms.append(self.arrived("early", 0, before))
        add_all(out, terms)
        self.send(("early", 0, k))

    def ending(self, kind, out, half, extra, panel):
        for part in range(2):
            terms = [self.stage(kind, half, 0, part)]
            terms += [self.arrived(kind, half, 1 + 3 * part), self.arrived(kind, half, 2 + 3 * part)]
            terms.append(extra(part)) if extra else None
            start, rows = self.window(kind, part)
            if panel is None:
                add_all(self.last(0, part), terms)
            else:
                add_all(out.at[pl.ds(start, rows)], terms, panel.at[pl.ds(start, rows)])

    def run(self, place, panel, dst):
        at = self.at
        order = (3, 1, 2, 0)

        def give(s):
            for half in range(2):
                self.send(("pair", half, s))

        def step(index):
            core = jnp.where(lax.rem(index, 2) == 0, 1 - at.core, at.core)
            row = choose(index // 2, [at.ring[s] for s in order])
            place([((half * 2 + core) * 4 + row) * self.block for half in range(2)], self.block)

        def second():
            give(1)
            self.total(3)
            self.late_out(0, 3)

        def fifth():
            self.land(("cross", 0, 3))
            self.early_out(0)
            self.early_out(3)

        def fourth():
            give(2)
            self.total(1)
            self.late_out(1)

        def sixth():
            give(0)
            self.total(2)
            self.late_out(4)
            self.late_next(0, 2)
            self.late_next(3, 5)

        after = {0: lambda: give(3), 2: second, 4: fourth, 5: fifth, 6: sixth}
        stepped(8, {}, step, after)
        self.total(0)
        self.land(("cross", 0, 1))
        self.early_out(1)
        self.land(("cross", 0, 2))
        self.early_out(4)
        self.early_out(2, 0)
        self.early_out(5, 3)
        for half in range(2):
            for k in (1, 4, 2, 5):
                self.land(("late", half, k))
        self.ending("late", None, 1 - at.upper, None, None)
        self.send(("last", 0, 0))
        self.land(("cross", 0, 0))
        for k in (1, 4, 2, 5):
            self.land(("early", 0, k))
        self.ending("early", dst, at.upper, lambda part: self.crossed(0, part), panel)
        self.land(("last", 0, 0))
        self.ending("late", dst, at.upper, lambda part: self.last(1, part), panel)
        self.finish()


def panel_kernel(
    low_hbm, mid_hbm, top_hbm, inv_low_hbm, inv_mid_hbm, inv_top_hbm, cpl_low_hbm, cpl_mid_hbm,
    parents_low_hbm, parents_mid_hbm,
    out_low, out_mid, out_top,
    inv_low, inv_mid, inv_top, cpl_low, cpl_mid, panel_mid, panel_top, parents_low, parents_mid,
    buf_a, buf_b, buf_c, buf_t, row_buf, z_buf, part, picked, wide,
    load, *sems,
):
    at = Place(4, 2)
    pulls = {}
    order = [
        ("low", low_hbm, rows_at(buf_a, at.row * low_hbm.shape[0], low_hbm.shape[0])),
        ("parents_low", parents_low_hbm, parents_low),
        ("parents_mid", parents_mid_hbm, parents_mid),
        ("inv_low", inv_low_hbm, inv_low),
        ("cpl_low", cpl_low_hbm, cpl_low),
        ("panel_mid", mid_hbm, panel_mid),
        ("inv_mid", inv_mid_hbm, inv_mid),
        ("cpl_mid", cpl_mid_hbm, cpl_mid),
        ("panel_top", top_hbm, panel_top),
        ("inv_top", inv_top_hbm, inv_top),
    ]
    for index, (name, src, dst) in enumerate(order):
        pulls[name] = pltpu.make_async_copy(src, dst, load.at[index])

    def need(*names):
        for name in names:
            pulls.pop(name).wait()

    for name in ("parents_low", "parents_mid", "low", "inv_low"):
        pulls[name].start()
    at.greet()
    low_sems, mid_sems, mid_sems2, top_sems, top_sems2, low_red, top_red = (
        sems[0:6], sems[6:12], sems[12:18], sems[18:24], sems[24:30], sems[30:36], sems[36:42]
    )
    need("low")
    low = Exchange(at, buf_a, 0, low_sems)
    for piece in low.pieces():
        low.begin(*piece)
    need("parents_low", "parents_mid")
    low_targets = parents_low[pl.ds(at.group, 1), :]
    mid_targets = parents_mid[pl.ds(at.group // 2, 1), :]
    spread_lanes(wide, mid_targets)
    for total in (out_low, out_mid, out_top, picked):
        total[...] = jnp.zeros_like(total)
    need("inv_low")
    for copy in pulls.values():
        copy.start()

    def user(matrix, panel, total, sign):
        def use(starts, depth):
            for start in starts:
                multiply(matrix, panel, total, start, depth, sign)

        return use

    def picker(panel):
        return lambda starts, depth: pick_add(picked, wide, panel, starts, depth)

    def placer(targets):
        return lambda starts, count: place_rows(buf_t, part, targets, starts, count)

    def begin(exchange, rows):
        for half, index in exchange.pieces():
            start, count = (half * exchange.sub + index) * exchange.count, exchange.count
            rows_at(exchange.buf, exchange.mine + start, count)[...] = rows(start, count).astype(jnp.bfloat16)
            exchange.begin(half, index)

    low.run(user(inv_low, buf_a, out_low, 1))

    need("cpl_low")
    couple_rows(cpl_low, out_low[...].astype(jnp.bfloat16), part)
    mid = Exchange(at, buf_b, 1, mid_sems)
    reduce_mid = Reduce(at, 1, buf_t, half_of(buf_c, 1), half_of(buf_c, 0), row_buf, z_buf, low_red)
    need("panel_mid")
    reduce_mid.run(placer(low_targets), panel_mid, rows_at(buf_b, mid.mine, mid.block))
    mid.begin(0)
    mid.begin(1)
    need("inv_mid")
    mid.run(user(inv_mid, buf_b, out_mid, 1))

    need("cpl_mid")
    couple_rows(cpl_mid, out_mid[...].astype(jnp.bfloat16), part)
    top = Exchange(at, buf_c, 2, top_sems)
    reduce_top = ReduceTwo(at, buf_t, half_of(buf_a, 0), half_of(buf_b, 0), row_buf, z_buf, top_red)
    need("panel_top")
    reduce_top.run(placer(mid_targets), panel_top, rows_at(buf_c, top.mine, top.block))
    top.begin(0)
    top.begin(1)
    need("inv_top")
    top.run(user(inv_top, buf_c, out_top, 1))

    back = Exchange(at, buf_t, 2, top_sems2)
    begin(back, lambda start, count: out_top[pl.ds(start, count), :])
    back.run(picker(buf_t))

    part[...] = picked[...].astype(jnp.bfloat16)
    lift = Exchange(at, buf_b, 1, mid_sems)
    begin(lift, lambda start, count: lift_rows(cpl_mid, part[...], start, count))
    spread_lanes(wide, low_targets)
    picked[...] = jnp.zeros_like(picked)
    lift.run(user(inv_mid, buf_b, out_mid, -1))

    back = Exchange(at, buf_c, 1, mid_sems2)
    begin(back, lambda start, count: out_mid[pl.ds(start, count), :])
    back.run(picker(buf_c))

    part[...] = picked[...].astype(jnp.bfloat16)
    lift = Exchange(at, buf_a, 0, low_sems)
    begin(lift, lambda start, count: lift_rows(cpl_low, part[...], start, count))
    lift.run(user(inv_low, buf_a, out_low, -1))


def settle_kernel(*refs):
    count = (len(refs) - 2) // 3
    sources, targets, held = refs[:count], refs[count : 2 * count], refs[2 * count : 3 * count]
    inward, outward = refs[3 * count :]
    pulls = [pltpu.make_async_copy(sources[i], held[i], inward.at[i]) for i in range(count)]
    pushes = [pltpu.make_async_copy(held[i], targets[i], outward.at[i]) for i in range(count)]
    for pull in pulls:
        pull.start()
    for pull, out in zip(pulls, pushes):
        pull.wait()
        out.start()
    for out in pushes:
        out.wait()


def settle(*arrays):
    count = len(arrays)
    return pl.pallas_call(
        settle_kernel,
        out_shape=tuple(jax.ShapeDtypeStruct(a.shape, a.dtype) for a in arrays),
        in_specs=[HBM_SPEC] * count,
        out_specs=(HBM_SPEC,) * count,
        scratch_shapes=[pltpu.VMEM(a.shape, a.dtype) for a in arrays] + [dma(count), dma(count)],
    )(*arrays)


def gather_sems(levels):
    units = 2 if levels >= 2 else 1
    return [dma(units, 12 if levels == 0 else 6)] * 2 + [dma(units, 8)] * 2 + [dma(2), dma(2)]


def reduce_sems(levels):
    pairs = [dma(levels, 4)] * 2
    return pairs + ([dma(3, 6)] * 2 + [dma(5)] * 2 if levels == 2 else [dma(1, 6)] * 2 + [dma(1)] * 2)


def solve_panel(
    panel_low, panel_mid, panel_top, inverse_low, inverse_mid, inverse_top, couple_low, couple_mid,
    parents_low, parents_mid,
):
    width = panel_low.shape[1]
    front, links = inverse_low.shape[2], couple_low.shape[1]

    def vmem(*shape, kind=jnp.bfloat16):
        return pltpu.VMEM(shape, kind)

    scratch = [vmem(*m.shape) for m in (inverse_low, inverse_mid, inverse_top, couple_low, couple_mid)]
    scratch += [vmem(*panel_mid.shape), vmem(*panel_top.shape)]
    scratch += [vmem(*parents.shape, kind=parents.dtype) for parents in (parents_low, parents_mid)]
    scratch += [vmem(front, width)] * 4
    scratch += [vmem(front * 3 // 8, width), vmem(4 * panel_top.shape[0], width)]
    scratch += [vmem(links, width), vmem(links, width, kind=jnp.float32)]
    scratch += [vmem(links, 128, kind=jnp.int32), dma(10)]
    scratch += gather_sems(0) + gather_sems(1) * 2 + gather_sems(2) * 2
    scratch += reduce_sems(1) + reduce_sems(2)
    solved = pl.pallas_call(
        panel_kernel,
        out_shape=tuple(
            jax.ShapeDtypeStruct(p.shape, jnp.float32) for p in (panel_low, panel_mid, panel_top)
        ),
        in_specs=[HBM_SPEC] * 10,
        out_specs=(VMEM_SPEC,) * 3,
        scratch_shapes=scratch,
        compiler_params=params(7, 63),
    )(
        panel_low, panel_mid, panel_top, inverse_low, inverse_mid, inverse_top, couple_low, couple_mid,
        parents_low, parents_mid,
    )
    return settle(*solved)


def on_device(
    n,
    panel_low,
    panel_mid,
    panel_top,
    inverse_low,
    inverse_mid,
    inverse_top,
    couple_low,
    couple_mid,
    parents_low,
    parents_mid,
):
    if n == 4:
        return solve_panel(
            panel_low, panel_mid, panel_top, inverse_low, inverse_mid, inverse_top, couple_low, couple_mid,
            parents_low, parents_mid,
        )
    group = lax.axis_index("grp")
    low_targets = lax.dynamic_index_in_dim(parents_low, group, 0, keepdims=False)
    mid_targets = lax.dynamic_index_in_dim(parents_mid, group // 2, 0, keepdims=False)
    low_y = gather_solve(panel_low, inverse_low, n, 0, 0)
    term = spread_rows(complex_product(couple_low, low_y.astype(jnp.bfloat16)), low_targets)
    mid_y = reduce_solve(term, panel_mid, inverse_mid, n, 1, 1)
    term = spread_rows(complex_product(couple_mid, mid_y.astype(jnp.bfloat16)), mid_targets)
    top_x = reduce_solve(term, panel_top, inverse_top, n, 2, 2)
    top_full = gather(top_x.astype(jnp.bfloat16), n, 2, 3)
    lift = transposed_product(couple_mid, pick_rows(top_full, mid_targets)).astype(jnp.bfloat16)
    mid_x = mid_y - gather_solve(lift, inverse_mid, n, 1, 4)
    mid_full = gather(mid_x.astype(jnp.bfloat16), n, 1, 5)
    lift = transposed_product(couple_low, pick_rows(mid_full, low_targets)).astype(jnp.bfloat16)
    low_x = low_y - gather_solve(lift, inverse_low, n, 0, 6)
    return (low_x, mid_x, top_x)


def solution(mesh):
    placed = (
        P(("grp", "row"), None),
        P(("grp", "row"), None),
        P(("grp", "row"), None),
        P(None, ("grp", "row"), None),
        P(None, ("grp", "row"), None),
        P(None, ("grp", "row"), None),
        P(None, None, ("grp", "row")),
        P(None, None, ("grp", "row")),
        P(),
        P(),
    )
    return jax.shard_map(
        functools.partial(on_device, mesh.shape["row"]),
        mesh=mesh,
        in_specs=placed,
        out_specs=(P(("grp", "row"), None), P(("grp", "row"), None), P(("grp", "row"), None)),
        check_vma=False,
    )
```
